512 devices in a mesh: req: 128 (over z, y, core), tp: 4 (over x).
Axes of the slice: x: 4, y: 8, z: 8, core: 2. Of those that a mesh axis runs over, the one named last changes fastest.
Arguments:
- hidden_in: bfloat16 [128, 128, 1024], P('req', 'tp'), may hold values from -6 to 6
- cache_keys: bfloat16 [128, 4096, 512], P('req', None, 'tp'), may hold values from -6 to 6
- cache_values: bfloat16 [128, 4096, 512], P('req', None, 'tp'), may hold values from -6 to 6
- lengths: int32 [128], replicated, may hold values from 0 to 4096, as said below
- request_order: int32 [128], replicated, may hold values from 0 to 127, each once
- routes: int32 [128, 128, 8], P('req'), may hold values from 0 to 31, all different within a row; in each aligned block of 32 rows (0 to 31, 32 to 63, ..., all dimensions but the last counted through in order) at most 12 rows name the same one
- query_weight: bfloat16 [1024, 1024], P(None, 'tp'), may hold values from -0.1875 to 0.1875
- key_weight: bfloat16 [1024, 512], P(None, 'tp'), may hold values from -0.1875 to 0.1875
- value_weight: bfloat16 [1024, 512], P(None, 'tp'), may hold values from -0.1875 to 0.1875
- out_weight: bfloat16 [1024, 1024], P('tp'), may hold values from -0.1875 to 0.1875
- attention_gain: float32 [1024], replicated, may hold values from 0.1 to 1.9
- expert_gain: float32 [1024], replicated, may hold values from 0.1 to 1.9
- router_weight: bfloat16 [1024, 32], replicated, may hold values from -0.1875 to 0.1875
- gate_weight: bfloat16 [128, 1024, 512], P('req', None, 'tp'), may hold values from -0.125 to 0.125, as said below
- up_weight: bfloat16 [128, 1024, 512], P('req', None, 'tp'), may hold values from -0.125 to 0.125, as said below
- down_weight: bfloat16 [128, 512, 1024], P('req', 'tp'), may hold values from -0.176776695 to 0.176776695, as said below
- final_gain: float32 [1024], replicated, may hold values from 0.1 to 1.9
- vocab_weight: bfloat16 [1024, 49152], P(None, ('req', 'tp')), may hold values from -0.1875 to 0.1875
Outputs:
- layer_out: bfloat16 [128, 128, 1024], P('req', 'tp')
- logits: float32 [128, 49152], P(None, ('req', 'tp'))
The draws below stay inside these ranges and needn't reach their ends.
Inputs may be any that keep to these rules, and one draw needn't show every extreme that they name: Slot r's cache holds valid keys and values at positions below lengths[r]; some slot's length is 4096. `request_order`: each request is held by exactly one slot. `routes`: each token names 8 different experts; in each aligned block of 32 tokens of a slot no expert is named by more than 12 tokens, and some expert reaches 12. `gate_weight`: stored copies k * 4 to k * 4 + 3 are equal and hold expert k. `up_weight`: stored copies k * 4 to k * 4 + 3 are equal and hold expert k. `down_weight`: stored copies k * 4 to k * 4 + 3 are equal and hold expert k.
All inputs are finite; a program needn't handle non-finite values.
Results may differ from the reference program's by a relative error of at most 0.015.
Values may be sent and summed in bfloat16 or wider, within the bound.
A program may use at most 64 MiB of HBM per device.

```python
import math
import jax
import jax.numpy as jnp
import numpy as np
from jax import lax

D = 1024
HEADS = 16
KV_HEADS = 8
HEAD_DIM = 64
EXPERTS = 32
EXPERT_FF = 512
TOPK = 8
VOCAB = 49152
SPAN = 128
CACHE_MAX = 4096
REQS = 128
REPL = 4
STORED = 128
BLOCK = 32
CAP = 12
N_TP = 4


def stored_experts(key, row_count, column_count, fan_in):
    drawn = jnp.clip(jax.random.normal(key, (EXPERTS, row_count, column_count), jnp.float32), -4.0, 4.0) * fan_in ** (-0.5)
    return jnp.repeat(drawn, STORED // EXPERTS, axis=0).astype(jnp.bfloat16)


def draw_gate_weight(key, part):
    return stored_experts(jax.random.fold_in(key, 11), D, EXPERT_FF, D)


def draw_up_weight(key, part):
    return stored_experts(jax.random.fold_in(key, 12), D, EXPERT_FF, D)


def draw_down_weight(key, part):
    return stored_experts(jax.random.fold_in(key, 13), EXPERT_FF, D, EXPERT_FF)


def draw_lengths(key, part):
    key_base, key_shape, key_pick = jax.random.split(jax.random.fold_in(key, 21), 3)
    uniform_part = jax.random.randint(key_base, (REQS,), 0, CACHE_MAX + 1)
    shape_part = jax.random.randint(key_shape, (REQS,), 0, CACHE_MAX + 1)
    skewed = uniform_part * shape_part // CACHE_MAX
    longest = jax.random.randint(key_pick, (), 0, REQS)
    return skewed.at[longest].set(CACHE_MAX).astype(jnp.int32)


def level_of(rng, shape, cuts, smallest, largest):
    gain, own = 1.0, jax.random.fold_in(rng, 6)
    for axis_at, parts in cuts:
        steps = jnp.exp(jax.random.uniform(jax.random.fold_in(own, axis_at), (parts,), jnp.float32, smallest / len(cuts), largest / len(cuts)))
        gain = gain * jnp.repeat(steps, shape[axis_at] // parts).reshape([-1 if axis == axis_at else 1 for axis in range(len(shape))])
    return gain


def deal_out(rng, own, number, rows, amount, top, most, slope):
    ranking = jax.random.permutation(rng, amount)
    crowded, ordinary = portions_of(amount, rows * top, most, slope, True), portions_of(amount, rows * top, most, slope, False)
    places = jnp.arange(amount)

    def named(sizes, rotation):
        used = int((sizes > 0).sum())
        fixed = max(1, used // 4)
        passed = fixed + (places - fixed + rotation * (used - fixed)) % max(1, amount - fixed)
        return jnp.zeros((amount,), jnp.int32).at[ranking[jnp.where(places < fixed, places, passed)]].set(jnp.asarray(sizes, jnp.int32))

    sizes = jnp.where(number % 4 == 0, named(crowded, number // 4), named(ordinary, number - number // 4 - 1))
    mixed = jax.random.permutation(jax.random.fold_in(own, 3), amount)
    donor, taker = mixed[0:amount // 2 * 2:2], mixed[1:amount // 2 * 2:2]
    margin = jnp.minimum(sizes[donor] - 1, most - sizes[taker]) // 2
    margin = jnp.where((donor == ranking[0]) | (taker == ranking[0]) | (sizes[taker] == 0), 0, jnp.maximum(margin, 0))
    passed = jax.random.randint(jax.random.fold_in(own, 4), (amount // 2,), 0, 1 << 20) % (margin + 1)
    sizes = sizes.at[donor].add(-passed).at[taker].add(passed)
    labels = jnp.searchsorted(jnp.cumsum(sizes), jnp.arange(rows * top), side="right").astype(jnp.int32)
    grid = labels.reshape(top, rows).T
    grid = grid[jax.random.permutation(jax.random.fold_in(own, 1), rows)]
    rotation = jax.random.randint(jax.random.fold_in(own, 2), (rows, 1), 0, top)
    return jnp.take_along_axis(grid, (jnp.arange(top)[None, :] + rotation) % top, axis=1)


def portions_of(number_of, total, reach, lean, full):
    weights = [(1 << 20) // math.isqrt(standing ** lean) + 1 for standing in range(1, number_of + 1)]
    largest = reach if full else min(reach, max(-(-total // number_of), total * weights[0] // sum(weights)))
    least = 1 if total - largest >= number_of - 1 else 0
    given, spare = [largest] + [least] * (number_of - 1), total - largest - least * (number_of - 1)
    while spare > 0:
        candidates = [i for i in range(1, number_of) if given[i] < largest] or [i for i in range(1, number_of) if given[i] < reach]
        pool, left = sum([weights[i] for i in candidates]), spare
        for i in candidates:
            extra = min(reach - given[i], max(1, left * weights[i] // pool), spare)
            given[i] = given[i] + extra
            spare = spare - extra
    return np.array(given)


def normal_values(own_key, shape, width, limit, cuts=(), held_as=jnp.bfloat16):
    factor_of = level_of(own_key, shape, cuts, -0.22, 0.18) if cuts else 1.0
    array = jax.random.normal(own_key, shape, jnp.float32) * width * factor_of
    return jnp.minimum(jnp.maximum(array, -limit), limit).astype(held_as)


def setup_inputs(seed: int = 0) -> dict:
    arg_keys = jax.random.split(jax.random.key(seed), 19)
    hidden_in = normal_values(arg_keys[0], (REQS, SPAN, D), 1.0, 6.0, ((0, 128), (1, 4)))
    cache_keys = normal_values(arg_keys[1], (REQS, CACHE_MAX, KV_HEADS * HEAD_DIM), 1.0, 6.0, ((0, 128), (2, 4)))
    cache_values = normal_values(arg_keys[2], (REQS, CACHE_MAX, KV_HEADS * HEAD_DIM), 1.0, 6.0, ((0, 128), (2, 4)))
    lengths = draw_lengths(jax.random.fold_in(arg_keys[18], 71), 0)
    request_order = jax.random.permutation(arg_keys[4], REQS).astype(jnp.int32)
    routes_keys = jax.random.split(jax.random.fold_in(arg_keys[5], 1), REQS * SPAN // BLOCK)
    routes_turns = jax.random.permutation(jax.random.fold_in(arg_keys[5], 3), REQS * SPAN // BLOCK)
    routes = jax.vmap(lambda own, number: deal_out(jax.random.fold_in(arg_keys[5], 2), own, number, BLOCK, EXPERTS, TOPK, CAP, 2))(routes_keys, routes_turns).reshape((REQS, SPAN, TOPK))
    query_weight = normal_values(arg_keys[6], (D, HEADS * HEAD_DIM), D ** -0.5, 0.1875, ((1, 4),))
    key_weight = normal_values(arg_keys[7], (D, KV_HEADS * HEAD_DIM), D ** -0.5, 0.1875, ((1, 4),))
    value_weight = normal_values(arg_keys[8], (D, KV_HEADS * HEAD_DIM), D ** -0.5, 0.1875, ((1, 4),))
    out_weight = normal_values(arg_keys[9], (HEADS * HEAD_DIM, D), (HEADS * HEAD_DIM) ** -0.5, 0.1875, ((0, 4),))
    attention_gain = jnp.clip(1.0 + 0.18 * jax.random.normal(arg_keys[10], (D,), jnp.float32), 0.1, 1.9)
    expert_gain = jnp.clip(1.0 + 0.18 * jax.random.normal(arg_keys[11], (D,), jnp.float32), 0.1, 1.9)
    router_weight = normal_values(arg_keys[12], (D, EXPERTS), D ** -0.5, 0.1875)
    gate_weight = draw_gate_weight(jax.random.fold_in(arg_keys[18], 71), 0)
    up_weight = draw_up_weight(jax.random.fold_in(arg_keys[18], 71), 0)
    down_weight = draw_down_weight(jax.random.fold_in(arg_keys[18], 71), 0)
    final_gain = jnp.clip(1.0 + 0.18 * jax.random.normal(arg_keys[16], (D,), jnp.float32), 0.1, 1.9)
    vocab_weight = normal_values(arg_keys[17], (D, VOCAB), D ** -0.5, 0.1875, ((1, 512),))
    return {"hidden_in": hidden_in, "cache_keys": cache_keys, "cache_values": cache_values, "lengths": lengths, "request_order": request_order, "routes": routes, "query_weight": query_weight, "key_weight": key_weight, "value_weight": value_weight, "out_weight": out_weight, "attention_gain": attention_gain, "expert_gain": expert_gain, "router_weight": router_weight, "gate_weight": gate_weight, "up_weight": up_weight, "down_weight": down_weight, "final_gain": final_gain, "vocab_weight": vocab_weight}


epsilon = 1e-06

def rms_scale(row_block, gain_vector):
    widened = row_block.astype(jnp.float32)
    return widened * lax.rsqrt(lax.optimization_barrier(jnp.mean(widened * widened, axis=-1, keepdims=True)) + epsilon) * gain_vector

def rotate(values, positions):
    half_dim = values.shape[-1] // 2
    frequency = jnp.exp(-jnp.log(10000.0) * jnp.arange(half_dim, dtype=jnp.float32) * (2.0 / values.shape[-1]))
    angles = positions.astype(jnp.float32)[:, None] * frequency[None, :]
    cosine_table = jnp.cos(angles)[:, None, :]
    sine_table = jnp.sin(angles)[:, None, :]
    front_half = values[..., :half_dim]
    back_half = values[..., half_dim:]
    return jnp.concatenate([front_half * cosine_table - back_half * sine_table, back_half * cosine_table + front_half * sine_table], axis=-1)

def rounded(value):
    return lax.optimization_barrier(value.astype(jnp.bfloat16)).astype(jnp.float32)

def reference(hidden_in, cache_keys, cache_values, lengths, request_order, routes, query_weight, key_weight, value_weight, out_weight, attention_gain, expert_gain, router_weight, gate_weight, up_weight, down_weight, final_gain, vocab_weight):
    group_size = HEADS // KV_HEADS
    score_scale = HEAD_DIM ** (-0.5)
    gate_experts = gate_weight[::REPL].astype(jnp.float32)
    up_experts = up_weight[::REPL].astype(jnp.float32)
    down_experts = down_weight[::REPL].astype(jnp.float32).reshape(EXPERTS, N_TP, EXPERT_FF // N_TP, D)
    out_groups = out_weight.astype(jnp.float32).reshape(N_TP, HEADS * HEAD_DIM // N_TP, D)
    token_range = jnp.arange(SPAN, dtype=jnp.int32)
    causal = token_range[None, :] <= token_range[:, None]
    cache_range = jnp.arange(CACHE_MAX, dtype=jnp.int32)

    def one_request(request):
        token_rows, key_rows, value_rows, length, route_ids = request
        attn_in = rms_scale(token_rows, attention_gain).astype(jnp.bfloat16)
        positions = length + token_range
        queries = rounded(rotate(jnp.dot(attn_in, query_weight, preferred_element_type=jnp.float32).reshape(SPAN, HEADS, HEAD_DIM), positions))
        new_keys = rounded(rotate(jnp.dot(attn_in, key_weight, preferred_element_type=jnp.float32).reshape(SPAN, KV_HEADS, HEAD_DIM), positions))
        new_values = rounded(jnp.dot(attn_in, value_weight, preferred_element_type=jnp.float32)).reshape(SPAN, KV_HEADS, HEAD_DIM)
        every_key = jnp.concatenate([key_rows.astype(jnp.float32).reshape(CACHE_MAX, KV_HEADS, HEAD_DIM), new_keys], axis=0)
        every_value = jnp.concatenate([value_rows.astype(jnp.float32).reshape(CACHE_MAX, KV_HEADS, HEAD_DIM), new_values], axis=0)
        grouped = queries.reshape(SPAN, KV_HEADS, group_size, HEAD_DIM)
        scores = jnp.einsum('ckgd,jkd->ckgj', grouped, every_key) * score_scale
        visible = jnp.concatenate([jnp.broadcast_to((cache_range < length)[None, :], (SPAN, CACHE_MAX)), causal], axis=1)
        exp_scores = jnp.where(visible[:, None, None, :], jnp.exp(scores), 0.0)
        weights = rounded(exp_scores)
        numerator = jnp.einsum('ckgj,jkd->ckgd', weights, every_value)
        attended = rounded(numerator / lax.optimization_barrier(jnp.sum(exp_scores, axis=-1))[..., None])
        head_groups = attended.reshape(SPAN, N_TP, HEADS * HEAD_DIM // N_TP)
        head_terms = rounded(jnp.einsum('cnh,nhd->cnd', head_groups, out_groups))
        mixed_rows = (token_rows.astype(jnp.float32) + lax.optimization_barrier(jnp.sum(head_terms, axis=1))).astype(jnp.bfloat16)
        expert_in = rms_scale(mixed_rows, expert_gain).astype(jnp.bfloat16)
        router_logits = jnp.dot(expert_in, router_weight, preferred_element_type=jnp.float32)
        chosen = route_ids[:, :, None] == jnp.arange(EXPERTS, dtype=jnp.int32)
        picked = lax.optimization_barrier(jnp.sum(jnp.where(chosen, router_logits[:, None, :], 0.0), axis=-1))
        gate_expo = jnp.exp(picked)
        gate_values = rounded(gate_expo / lax.optimization_barrier(jnp.sum(gate_expo, axis=-1, keepdims=True)))
        counts = lax.optimization_barrier(jnp.sum(chosen.astype(jnp.int32), axis=1)).astype(jnp.int32)
        blocked = counts.reshape(REPL, BLOCK, EXPERTS)
        rank_table = (jnp.cumsum(blocked, axis=1) - blocked).astype(jnp.int32).reshape(SPAN, EXPERTS)
        rank_pick = lax.optimization_barrier(jnp.sum(jnp.where(chosen, rank_table[:, None, :], 0), axis=-1)).astype(jnp.int32)
        slot_ids = ((route_ids * REPL + (token_range // BLOCK)[:, None]) * CAP + rank_pick).astype(jnp.int32)
        slot_token = jnp.full((EXPERTS * REPL * CAP,), SPAN, jnp.int32).at[slot_ids.reshape(-1)].set(jnp.repeat(token_range, TOPK))
        gathered = jnp.take(expert_in, slot_token, axis=0, mode='fill', fill_value=0).astype(jnp.float32).reshape(EXPERTS, REPL * CAP, D)
        gate_part = jnp.einsum('esd,edf->esf', gathered, gate_experts)
        up_part = jnp.einsum('esd,edf->esf', gathered, up_experts)
        unit_hidden = rounded(jax.nn.silu(gate_part) * up_part).reshape(EXPERTS, REPL * CAP, N_TP, EXPERT_FF // N_TP)
        unit_terms = rounded(jnp.einsum('esnf,enfd->esnd', unit_hidden, down_experts))
        expert_out = rounded(lax.optimization_barrier(jnp.sum(unit_terms, axis=2))).reshape(EXPERTS * REPL * CAP, D)
        routed = jnp.take(expert_out, slot_ids, axis=0)
        moe_sum = lax.optimization_barrier(jnp.sum(gate_values[..., None] * routed, axis=1))
        layer_rows = (mixed_rows.astype(jnp.float32) + moe_sum).astype(jnp.bfloat16)
        return (layer_rows, layer_rows[SPAN - 1])
    layer_out, tail_rows = lax.map(one_request, (hidden_in, cache_keys, cache_values, lengths, routes))
    final_in = rms_scale(tail_rows, final_gain).astype(jnp.bfloat16)
    slot_logits = jnp.dot(final_in, vocab_weight, preferred_element_type=jnp.float32)
    logits = jnp.zeros_like(slot_logits).at[request_order].set(slot_logits)
    return (layer_out, logits)
```

```python
import functools

import jax
import jax.numpy as jnp
from jax.experimental import pallas as pl
from jax.experimental.pallas import tpu as pltpu
from jax import lax
from jax.sharding import PartitionSpec as P

HEAD_DIM = 64
EXPERTS = 32
TOPK = 8
SPAN = 128
SLOT_ROWS = 16
MESH = pl.DeviceIdType.MESH
VMEM_SPEC = pl.BlockSpec(memory_space=pltpu.VMEM)


epsilon = 1e-06
key_block = 512


def rms_scale(row_block, gain_vector):
    widened = row_block.astype(jnp.float32)
    return (
        widened
        * lax.rsqrt(jnp.mean(widened * widened, axis=-1, keepdims=True) + epsilon)
        * gain_vector
    )


def rotate(values, positions):
    half_dim = values.shape[-1] // 2
    frequency = jnp.exp(
        -jnp.log(10000.0) * jnp.arange(half_dim, dtype=jnp.float32) * (2.0 / values.shape[-1])
    )
    angles = positions.astype(jnp.float32)[:, None] * frequency[None, :]
    cosine_table = jnp.cos(angles)[:, None, :]
    sine_table = jnp.sin(angles)[:, None, :]
    front_half = values[..., :half_dim]
    back_half = values[..., half_dim:]
    return jnp.concatenate(
        [
            front_half * cosine_table - back_half * sine_table,
            back_half * cosine_table + front_half * sine_table,
        ],
        axis=-1,
    )


def cache_attend(queries, key_rows, value_rows, lowest, highest):
    token_count, key_heads, group_size, head_size = queries.shape
    window = min(key_block, key_rows.shape[0])
    score_scale = head_size ** (-0.5)

    def block_step(block_number, running):
        numerator, denominator = running
        offset = block_number * window
        block_keys = lax.dynamic_slice_in_dim(key_rows, offset, window, 0).reshape(
            window, key_heads, head_size
        )
        block_values = lax.dynamic_slice_in_dim(value_rows, offset, window, 0).reshape(
            window, key_heads, head_size
        )
        scores = (
            jnp.einsum("ckgd,jkd->ckgj", queries, block_keys, preferred_element_type=jnp.float32)
            * score_scale
        )
        key_places = offset + jnp.arange(window, dtype=jnp.int32)
        inside = (key_places >= lowest) & (key_places < highest)
        exp_scores = jnp.where(inside, jnp.exp(scores), 0.0)
        numerator = numerator + jnp.einsum(
            "ckgj,jkd->ckgd",
            exp_scores.astype(jnp.bfloat16),
            block_values,
            preferred_element_type=jnp.float32,
        )
        return (numerator, denominator + jnp.sum(exp_scores, axis=-1))

    first_block = lowest // window
    last_block = (highest + window - 1) // window
    initial = (
        jnp.zeros((token_count, key_heads, group_size, head_size), jnp.float32),
        jnp.zeros((token_count, key_heads, group_size), jnp.float32),
    )
    return lax.fori_loop(first_block, last_block, block_step, initial)


def send(source, target, send_sem, recv_sem, device):
    return pltpu.make_async_remote_copy(
        src_ref=source,
        dst_ref=target,
        send_sem=send_sem,
        recv_sem=recv_sem,
        device_id=device,
        device_id_type=MESH,
    )


def greet(barrier, device):
    pl.semaphore_signal(barrier, inc=1, device_id=device, device_id_type=MESH)


def lane_gather_kernel(lanes, own_ref, all_ref, send_sem, recv_sem, local_sem):
    req, me = lax.axis_index("req"), lax.axis_index("tp")
    rows = own_ref.shape[0]
    place = pl.ds(pl.multiple_of(me * rows, rows), rows)
    barrier = pltpu.get_barrier_semaphore()
    for step in range(1, lanes):
        greet(barrier, (req, lax.rem(me + step, lanes)))
    local = pltpu.make_async_copy(own_ref, all_ref.at[place], local_sem)
    local.start()
    pl.semaphore_wait(barrier, lanes - 1)
    copies = []
    for step in range(1, lanes):
        copy = send(
            own_ref,
            all_ref.at[place],
            send_sem.at[step - 1],
            recv_sem.at[step - 1],
            (req, lax.rem(me + step, lanes)),
        )
        copy.start()
        copies.append(copy)
    for copy in copies:
        copy.wait()
    local.wait()


def lane_gather(own, lanes):
    rows, width = own.shape
    return pl.pallas_call(
        functools.partial(lane_gather_kernel, lanes),
        out_shape=jax.ShapeDtypeStruct((lanes * rows, width), own.dtype),
        in_specs=[VMEM_SPEC],
        out_specs=VMEM_SPEC,
        scratch_shapes=[
            pltpu.SemaphoreType.DMA((lanes - 1,)),
            pltpu.SemaphoreType.DMA((lanes - 1,)),
            pltpu.SemaphoreType.DMA,
        ],
        compiler_params=pltpu.CompilerParams(collective_id=0, has_side_effects=True),
        name="lane_gather",
    )(own)


def mix_kernel(lanes, part_ref, own_ref, gain_ref, mixed_ref, expert_ref, held, send_sem, recv_sem):
    req, me = lax.axis_index("req"), lax.axis_index("tp")
    rows = own_ref.shape[0]
    barrier = pltpu.get_barrier_semaphore()
    for step in range(1, lanes):
        greet(barrier, (req, lax.rem(me + step, lanes)))
    pl.semaphore_wait(barrier, lanes - 1)
    copies = []
    for step in range(1, lanes):
        other = lax.rem(me + step, lanes)
        copy = send(
            part_ref.at[pl.ds(pl.multiple_of(other * rows, rows), rows)],
            held.at[step - 1],
            send_sem.at[step - 1],
            recv_sem.at[step - 1],
            (req, other),
        )
        copy.start()
        copies.append(copy)
    total = part_ref[pl.ds(pl.multiple_of(me * rows, rows), rows), :].astype(jnp.float32)
    for step, copy in enumerate(copies):
        copy.wait()
        total = total + held[step].astype(jnp.float32)
    mixed = (own_ref[...].astype(jnp.float32) + total).astype(jnp.bfloat16)
    mixed_ref[...] = mixed
    expert_ref[...] = rms_scale(mixed, gain_ref[...]).astype(jnp.bfloat16)


def mix_rows(partial_rows, own, gain, lanes):
    rows, width = own.shape
    return pl.pallas_call(
        functools.partial(mix_kernel, lanes),
        out_shape=[jax.ShapeDtypeStruct((rows, width), jnp.bfloat16)] * 2,
        in_specs=[VMEM_SPEC] * 3,
        out_specs=[VMEM_SPEC] * 2,
        scratch_shapes=[
            pltpu.VMEM((lanes - 1, rows, width), jnp.bfloat16),
            pltpu.SemaphoreType.DMA((lanes - 1,)),
            pltpu.SemaphoreType.DMA((lanes - 1,)),
        ],
        compiler_params=pltpu.CompilerParams(collective_id=1, has_side_effects=True),
        name="mix_rows",
    )(partial_rows, own, gain)


def expert_kernel(
    lanes,
    copies_of,
    group,
    out_ref,
    gate_ref,
    up_ref,
    down_ref,
    back_ref,
    arrived,
    result,
    gates,
    ups,
    downs,
    go_send,
    go_recv,
    ret_send,
    ret_recv,
    weight_send,
    weight_recv,
    local_sem,
):
    req, me = lax.axis_index("req"), lax.axis_index("tp")
    experts = out_ref.shape[0]
    width = out_ref.shape[2]
    mine, replica = req // copies_of, lax.rem(req, copies_of)
    barrier = pltpu.get_barrier_semaphore()

    def peer(step):
        return (lax.rem(mine + step, experts) * copies_of + replica, me)

    for step in range(1, lanes):
        greet(barrier, (req, lax.rem(me + step, lanes)))

    @pl.loop(1, experts)
    def _(step):
        greet(barrier, peer(step))

    own_block = pltpu.make_async_copy(out_ref.at[mine], arrived.at[0], local_sem.at[0])
    own_block.start()
    pl.semaphore_wait(barrier, lanes - 1 + experts - 1)

    def weight_copies():
        found = []
        for step in range(1, lanes):
            for number, (source, target) in enumerate(
                ((gate_ref, gates), (up_ref, ups), (down_ref, downs))
            ):
                found.append(
                    send(
                        source,
                        target.at[step - 1],
                        weight_send.at[step - 1, number],
                        weight_recv.at[step - 1, number],
                        (req, lax.rem(me + step, lanes)),
                    )
                )
        return found

    def go_copy(step):
        return send(
            out_ref.at[lax.rem(mine + step, experts)],
            arrived.at[step],
            go_send.at[step],
            go_recv.at[step],
            peer(step),
        )

    def return_copy(step):
        return send(
            result.at[step],
            back_ref.at[mine],
            ret_send.at[step],
            ret_recv.at[step],
            (lax.rem(mine + experts - step, experts) * copies_of + replica, me),
        )

    for copy in weight_copies():
        copy.start()

    @pl.loop(1, experts)
    def _(step):
        go_copy(step).start()

    own_block.wait()
    for copy in weight_copies():
        copy.wait()

    @pl.loop(0, experts // group)
    def _(number):
        first = number * group
        for offset in range(group):
            step = first + offset

            @pl.when(step > 0)
            def _():
                go_copy(step).wait_recv()

        rows = arrived[pl.ds(first, group)].reshape(group * SLOT_ROWS, width)
        total = None
        for lane in range(lanes):
            gate_block = gate_ref[...] if lane == 0 else gates[lane - 1]
            up_block = up_ref[...] if lane == 0 else ups[lane - 1]
            down_block = down_ref[...] if lane == 0 else downs[lane - 1]
            gate_part = jnp.dot(rows, gate_block, preferred_element_type=jnp.float32)
            up_part = jnp.dot(rows, up_block, preferred_element_type=jnp.float32)
            hidden = (gate_part / (1.0 + jnp.exp(-gate_part)) * up_part).astype(jnp.bfloat16)
            term = jnp.dot(hidden, down_block, preferred_element_type=jnp.float32)
            total = term if total is None else total + term
        result[pl.ds(first, group)] = total.astype(jnp.bfloat16).reshape(group, SLOT_ROWS, width)
        for offset in range(group):
            step = first + offset

            @pl.when(step > 0)
            def _():
                return_copy(step).start()

            @pl.when(step == 0)
            def _():
                pltpu.make_async_copy(
                    result.at[0], back_ref.at[mine], local_sem.at[1]
                ).start()

    pltpu.make_async_copy(result.at[0], back_ref.at[mine], local_sem.at[1]).wait()

    @pl.loop(1, experts)
    def _(step):
        go_copy(step).wait_send()
        return_copy(step).wait()


def expert_exchange(outgoing, gate, up, down, lanes, copies_of):
    experts, slot_rows, width = outgoing.shape
    units = gate.shape[1]
    held = pltpu.VMEM((experts, slot_rows, width), jnp.bfloat16)
    return pl.pallas_call(
        functools.partial(expert_kernel, lanes, copies_of, 8),
        out_shape=jax.ShapeDtypeStruct((experts, slot_rows, width), jnp.bfloat16),
        in_specs=[VMEM_SPEC] * 4,
        out_specs=VMEM_SPEC,
        scratch_shapes=[
            held,
            held,
            pltpu.VMEM((lanes - 1, width, units), jnp.bfloat16),
            pltpu.VMEM((lanes - 1, width, units), jnp.bfloat16),
            pltpu.VMEM((lanes - 1, units, width), jnp.bfloat16),
            pltpu.SemaphoreType.DMA((experts,)),
            pltpu.SemaphoreType.DMA((experts,)),
            pltpu.SemaphoreType.DMA((experts,)),
            pltpu.SemaphoreType.DMA((experts,)),
            pltpu.SemaphoreType.DMA((lanes - 1, 3)),
            pltpu.SemaphoreType.DMA((lanes - 1, 3)),
            pltpu.SemaphoreType.DMA((2,)),
        ],
        compiler_params=pltpu.CompilerParams(collective_id=2, has_side_effects=True),
        name="expert_exchange",
    )(outgoing, gate, up, down)


def tail_kernel(
    lanes,
    near,
    far,
    tail_ref,
    gain_ref,
    order_ref,
    vocab_ref,
    logits_ref,
    rows_ref,
    lane_send,
    lane_recv,
    near_send,
    near_recv,
    far_send,
    far_recv,
    local_sem,
):
    req, me = lax.axis_index("req"), lax.axis_index("tp")
    plane, place = req // near, lax.rem(req, near)
    last = lanes - 1
    barrier = pltpu.get_barrier_semaphore()
    for step in range(1, lanes):
        greet(barrier, (req, lax.rem(me + step, lanes)))
    for step in range(1, near):
        greet(barrier, (plane * near + lax.rem(place + step, near), me))
    for step in range(1, far):
        greet(barrier, (lax.rem(plane + step, far) * near + place, me))
    pl.semaphore_wait(barrier, lanes - 1 + near - 1 + far - 1)

    @pl.when(me == last)
    def _():
        own = pltpu.make_async_copy(tail_ref, rows_ref.at[req], local_sem)
        own.start()
        copies = [
            send(tail_ref, rows_ref.at[req], lane_send.at[lane], lane_recv, (req, lane))
            for lane in range(last)
        ]
        for copy in copies:
            copy.start()
        own.wait()
        for copy in copies:
            copy.wait_send()

    @pl.when(me != last)
    def _():
        send(tail_ref, rows_ref.at[req], lane_send.at[0], lane_recv, (req, last)).wait_recv()

    copies = []
    for step in range(1, near):
        copy = send(
            rows_ref.at[req],
            rows_ref.at[req],
            near_send.at[step - 1],
            near_recv.at[step - 1],
            (plane * near + lax.rem(place + step, near), me),
        )
        copy.start()
        copies.append(copy)
    for copy in copies:
        copy.wait()
    copies = []
    block = pl.ds(plane * near, near)
    for step in range(1, far):
        copy = send(
            rows_ref.at[block],
            rows_ref.at[block],
            far_send.at[step - 1],
            far_recv.at[step - 1],
            (lax.rem(plane + step, far) * near + place, me),
        )
        copy.start()
        copies.append(copy)
    for copy in copies:
        copy.wait()

    count, parts, lanes_wide = rows_ref.shape
    square = jnp.zeros((count, 1), jnp.float32)
    for part in range(parts):
        piece = rows_ref[:, part, :]
        square = square + jnp.sum(piece * piece, axis=-1, keepdims=True)
    scale = lax.rsqrt(square / (parts * lanes_wide) + epsilon)
    chosen = (
        lax.broadcasted_iota(jnp.int32, (count, count), 0) == order_ref[...]
    ).astype(jnp.bfloat16)
    total = jnp.zeros(logits_ref.shape, jnp.float32)
    for part in range(parts):
        final = (rows_ref[:, part, :] * scale * gain_ref[part, :][None, :]).astype(jnp.bfloat16)
        ordered = jnp.dot(chosen, final, preferred_element_type=jnp.float32).astype(jnp.bfloat16)
        total = total + jnp.dot(
            ordered,
            vocab_ref[part * lanes_wide : (part + 1) * lanes_wide, :],
            preferred_element_type=jnp.float32,
        )
    logits_ref[...] = total


def tail_logits(tail, gain, order, vocab, lanes):
    reqs = order.shape[1]
    near = 16 if reqs % 16 == 0 else reqs
    far = reqs // near
    parts, wide = tail.shape
    return pl.pallas_call(
        functools.partial(tail_kernel, lanes, near, far),
        out_shape=jax.ShapeDtypeStruct((reqs, vocab.shape[1]), jnp.float32),
        in_specs=[VMEM_SPEC] * 4,
        out_specs=VMEM_SPEC,
        scratch_shapes=[
            pltpu.VMEM((reqs, parts, wide), jnp.float32),
            pltpu.SemaphoreType.DMA((lanes - 1,)),
            pltpu.SemaphoreType.DMA,
            pltpu.SemaphoreType.DMA((near - 1,)),
            pltpu.SemaphoreType.DMA((near - 1,)),
            pltpu.SemaphoreType.DMA((far - 1,)),
            pltpu.SemaphoreType.DMA((far - 1,)),
            pltpu.SemaphoreType.DMA,
        ],
        compiler_params=pltpu.CompilerParams(collective_id=3, has_side_effects=True),
        name="tail_logits",
    )(tail, gain, order, vocab)


def body(
    hidden_in,
    cache_keys,
    cache_values,
    lengths,
    request_order,
    routes,
    query_weight,
    key_weight,
    value_weight,
    out_weight,
    attention_gain,
    expert_gain,
    router_weight,
    gate_weight,
    up_weight,
    down_weight,
    final_gain,
    vocab_weight,
):
    lane_count = lax.axis_size("tp")
    req_count = lax.axis_size("req")
    lane_index = lax.axis_index("tp")
    slot_index = lax.axis_index("req")
    own_rows = hidden_in[0]
    shard_rows = own_rows.shape[0]
    model_width = own_rows.shape[1]
    query_width = query_weight.shape[1]
    key_width = key_weight.shape[1]
    key_heads = key_width // HEAD_DIM
    group_size = query_width // key_width
    attn_in = rms_scale(own_rows, attention_gain).astype(jnp.bfloat16)
    joined = jnp.concatenate([query_weight, key_weight, value_weight], axis=1)
    projected = jnp.dot(
        lane_gather(attn_in, lane_count),
        joined,
        preferred_element_type=jnp.float32,
    )
    my_length = lengths[slot_index]
    positions = my_length + jnp.arange(SPAN, dtype=jnp.int32)
    queries = (
        rotate(
            projected[:, :query_width].reshape(SPAN, key_heads * group_size, HEAD_DIM), positions
        )
        .astype(jnp.bfloat16)
        .reshape(SPAN, key_heads, group_size, HEAD_DIM)
    )
    new_keys = rotate(
        projected[:, query_width : query_width + key_width].reshape(SPAN, key_heads, HEAD_DIM),
        positions,
    ).astype(jnp.bfloat16)
    new_values = (
        projected[:, query_width + key_width :]
        .astype(jnp.bfloat16)
        .reshape(SPAN, key_heads, HEAD_DIM)
    )
    score_scale = HEAD_DIM ** (-0.5)
    token_range = jnp.arange(SPAN, dtype=jnp.int32)
    causal = token_range[None, :] <= token_range[:, None]
    span_scores = (
        jnp.einsum("ckgd,jkd->ckgj", queries, new_keys, preferred_element_type=jnp.float32)
        * score_scale
    )
    span_expo = jnp.where(causal[:, None, None, :], jnp.exp(span_scores), 0.0)
    numerator = jnp.einsum(
        "ckgj,jkd->ckgd",
        span_expo.astype(jnp.bfloat16),
        new_values,
        preferred_element_type=jnp.float32,
    )
    denominator = jnp.sum(span_expo, axis=-1)
    own_keys = cache_keys[0]
    own_values = cache_values[0]
    own_numer, own_denom = cache_attend(queries, own_keys, own_values, 0, my_length)
    numerator = numerator + own_numer
    denominator = denominator + own_denom
    attended = (numerator / denominator[..., None]).astype(jnp.bfloat16).reshape(SPAN, query_width)
    head_rows = jnp.dot(attended, out_weight, preferred_element_type=jnp.float32).astype(
        jnp.bfloat16
    )
    mixed_rows, expert_in = mix_rows(
        head_rows, own_rows, expert_gain.reshape(1, model_width), lane_count
    )
    router_logits = jnp.dot(expert_in, router_weight, preferred_element_type=jnp.float32)
    route_ids = lax.dynamic_slice_in_dim(routes[0], lane_index * shard_rows, shard_rows, 0)
    expert_range = jnp.arange(EXPERTS, dtype=jnp.int32)
    named = jnp.any(route_ids[:, :, None] == expert_range, axis=1)
    gate_expo = jnp.where(named, jnp.exp(router_logits), 0.0)
    gate_values = (gate_expo / jnp.sum(gate_expo, axis=-1, keepdims=True)).astype(jnp.bfloat16)
    counts = named.astype(jnp.int32)
    ranks = jnp.where(named, jnp.cumsum(counts, axis=0) - 1, -1)
    place = ranks.T[:, None, :] == jnp.arange(SLOT_ROWS, dtype=jnp.int32)[None, :, None]
    picker = place.astype(jnp.bfloat16).reshape(EXPERTS * SLOT_ROWS, shard_rows)
    combine = jnp.where(place, gate_values.T[:, None, :], jnp.zeros((), jnp.bfloat16)).reshape(
        EXPERTS * SLOT_ROWS, shard_rows
    )
    outgoing = (
        jnp.dot(picker, expert_in, preferred_element_type=jnp.float32)
        .astype(jnp.bfloat16)
        .reshape(EXPERTS, SLOT_ROWS, model_width)
    )
    returned = expert_exchange(
        outgoing, gate_weight[0], up_weight[0], down_weight[0], lane_count, req_count // EXPERTS
    )
    expert_sum = lax.dot_general(
        combine,
        returned.reshape(EXPERTS * SLOT_ROWS, model_width),
        (((0,), (0,)), ((), ())),
        preferred_element_type=jnp.float32,
    )
    layer_rows = (mixed_rows.astype(jnp.float32) + expert_sum).astype(jnp.bfloat16)
    tail_row = layer_rows[shard_rows - 1].astype(jnp.float32).reshape(model_width // 128, 128)
    logits = tail_logits(
        tail_row,
        final_gain.reshape(model_width // 128, 128),
        request_order.reshape(1, req_count),
        vocab_weight,
        lane_count,
    )
    return (layer_rows[None], logits)


def solution(mesh):
    in_specs = (
        P("req", "tp", None),
        P("req", None, "tp"),
        P("req", None, "tp"),
        P(),
        P(),
        P("req", None, None),
        P(None, "tp"),
        P(None, "tp"),
        P(None, "tp"),
        P("tp", None),
        P(),
        P(),
        P(),
        P("req", None, "tp"),
        P("req", None, "tp"),
        P("req", "tp", None),
        P(),
        P(None, ("req", "tp")),
    )
    out_specs = (P("req", "tp", None), P(None, ("req", "tp")))
    return jax.shard_map(body, mesh=mesh, in_specs=in_specs, out_specs=out_specs, check_vma=False)
```

```python
import jax
import jax.numpy as jnp
from jax.experimental import pallas as pl
from jax.experimental.pallas import tpu as pltpu
from jax import lax
from jax.sharding import PartitionSpec as P

HEAD_DIM = 64
EXPERTS = 32
TOPK = 8
LANES = 4
RING_Y = 8
RING_Z = 8
SPAN = 128
SLOT_ROWS = 16
CAP = 12
PACKED = 768
CHUNK = 256
MESH = pl.DeviceIdType.MESH
VMEM_SPEC = pl.BlockSpec(memory_space=pltpu.VMEM)


epsilon = 1e-06
key_block = 512
float32 = jnp.float32
bfloat16 = jnp.bfloat16


def rms_scale(row_block, gain_vector):
    widened = row_block.astype(jnp.float32)
    return (
        widened
        * lax.rsqrt(jnp.mean(widened * widened, axis=-1, keepdims=True) + epsilon)
        * gain_vector
    )


def send(source, target, send_sem, recv_sem, device):
    return pltpu.make_async_remote_copy(
        src_ref=source,
        dst_ref=target,
        send_sem=send_sem,
        recv_sem=recv_sem,
        device_id=device,
        device_id_type=MESH,
    )


def greet(barrier, device):
    pl.semaphore_signal(barrier, inc=1, device_id=device, device_id_type=MESH)


def dot(a, b):
    return jnp.dot(a, b, preferred_element_type=float32)


def dot_last(a, b):
    return lax.dot_general(a, b, (((1,), (1,)), ((), ())), preferred_element_type=float32)


def iota(shape, axis):
    return lax.broadcasted_iota(jnp.int32, shape, axis)


def one_hot(mask):
    return jnp.where(mask, 1.0, 0.0).astype(bfloat16)


def packed_rank(slot_row, chunk):
    if chunk is None:
        return jnp.where(slot_row < CAP, slot_row, -1)
    return jnp.where(slot_row >= CAP, slot_row - CAP + (SLOT_ROWS - CAP) * chunk, -1)


def layer_kernel(
    length_ref,
    own_ref,
    keys_ref,
    values_ref,
    table_ref,
    routes_ref,
    query_ref,
    key_ref,
    value_ref,
    out_ref,
    attention_gain_ref,
    expert_gain_ref,
    router_ref,
    gate_ref,
    up_ref,
    down_ref,
    final_gain_ref,
    order_ref,
    vocab_ref,
    layer_ref,
    logits_ref,
    normed,
    all_rows,
    stacked,
    numerator,
    denominator,
    part,
    part_held,
    outgoing,
    arrived,
    result,
    back,
    gates,
    ups,
    downs,
    tail,
    tails,
    tails_wide,
    row_send,
    row_recv,
    mix_send,
    mix_recv,
    weight_send,
    weight_recv,
    go_send,
    go_recv,
    ret_send,
    ret_recv,
    lane_send,
    lane_recv,
    plane_send,
    plane_recv,
    core_sem,
    local_sem,
):
    req, me = lax.axis_index("req"), lax.axis_index("tp")
    z, y, core = req // (2 * RING_Y), lax.rem(req // 2, RING_Y), lax.rem(req, 2)
    place = req // 2
    places = RING_Y * RING_Z
    mine = place // 2
    experts, _, _ = outgoing.shape
    rows, width = own_ref.shape
    partner = z * 2 * RING_Y + y * 2 + 1 - core
    last = LANES - 1
    barrier = pltpu.get_barrier_semaphore()

    def lane(step):
        return (req, lax.rem(me + step, LANES))

    def plane_peer(step):
        return (lax.rem(place + step, places) * 2 + core, me)

    for step in range(1, LANES):
        greet(barrier, lane(step))
    greet(barrier, (partner, me))

    @pl.loop(1, places)
    def _(step):
        greet(barrier, plane_peer(step))

    normed[...] = rms_scale(own_ref[...], attention_gain_ref[...]).astype(bfloat16)
    own_place = pl.ds(pl.multiple_of(me * rows, rows), rows)
    local = pltpu.make_async_copy(normed, all_rows.at[own_place], local_sem.at[0])
    local.start()
    pl.semaphore_wait(barrier, LANES - 1 + 1 + places - 1)

    row_copies = [
        send(normed, all_rows.at[own_place], row_send.at[step - 1], row_recv.at[step - 1], lane(step))
        for step in range(1, LANES)
    ]
    for copy in row_copies:
        copy.start()
    triples = ((gate_ref, gates), (up_ref, ups), (down_ref, downs))

    def near_weights():
        return [
            send(
                source,
                target.at[side],
                weight_send.at[side, number],
                weight_recv.at[side, number],
                lane((1, LANES - 1)[side]),
            )
            for number, (source, target) in enumerate(triples)
            for side in range(2)
        ]

    def far_weights():
        found = []
        for number, (source, target) in enumerate(triples):
            half = source.shape[0] // 2
            for side in range(2):
                piece = pl.ds(side * half, half)
                found.append(
                    send(
                        target.at[side, piece],
                        target.at[2, piece],
                        weight_send.at[2 + side, number],
                        weight_recv.at[2 + side, number],
                        lane((1, LANES - 1)[side]),
                    )
                )
        return found

    for copy in near_weights():
        copy.start()
    for copy in row_copies:
        copy.wait()
    local.wait()

    lanes_at = iota((SPAN, 128), 1)
    front = lax.rem(lanes_at, HEAD_DIM) < HEAD_DIM // 2
    first_head = lanes_at < HEAD_DIM
    cosine, sine = table_ref[0], table_ref[1]
    token_rows = all_rows[...]

    def turned(piece):
        other = jnp.where(
            front, -pltpu.roll(piece, 128 - HEAD_DIM // 2, 1), pltpu.roll(piece, HEAD_DIM // 2, 1)
        )
        return piece * cosine + other * sine

    projected = dot(token_rows, query_ref[...])
    zero = jnp.zeros((SPAN, 128), float32)
    for group in range(2):
        piece = turned(projected[:, group * 128 : (group + 1) * 128]).astype(bfloat16).astype(float32)
        piece = piece * HEAD_DIM ** (-0.5)
        swapped = pltpu.roll(piece, HEAD_DIM, 1)
        keep = first_head if group == 0 else jnp.logical_not(first_head)
        pair = (piece, swapped) if group == 0 else (swapped, piece)
        for member in range(2):
            at = (group * 2 + member) * SPAN
            stacked[at : at + SPAN, :] = jnp.where(keep, pair[member], zero).astype(bfloat16)
    new_keys = turned(dot(token_rows, key_ref[...])).astype(bfloat16)
    new_values = dot(token_rows, value_ref[...]).astype(bfloat16)
    heads = 4 * SPAN
    causal = iota((heads, SPAN), 1) <= lax.rem(iota((heads, SPAN), 0), SPAN)
    expo = jnp.where(causal, jnp.exp(dot_last(stacked[...], new_keys)), 0.0)
    numerator[...] = dot(expo.astype(bfloat16), new_values)
    denominator[...] = jnp.sum(expo, axis=-1, keepdims=True)
    length = length_ref[req]

    @pl.loop(0, keys_ref.shape[0] // key_block)
    def _(number):
        at = pl.ds(pl.multiple_of(number * key_block, key_block), key_block)
        scores = dot_last(stacked[...], keys_ref[at, :])
        inside = iota((heads, key_block), 1) < length - number * key_block
        block = jnp.where(inside, jnp.exp(scores), 0.0)
        numerator[...] += dot(block.astype(bfloat16), values_ref[at, :])
        denominator[...] += jnp.sum(block, axis=-1, keepdims=True)

    mean_values = numerator[...] / denominator[...]
    head = [mean_values[at * SPAN : (at + 1) * SPAN] for at in range(4)]
    attended = jnp.concatenate(
        [
            jnp.where(first_head, head[0], pltpu.roll(head[1], HEAD_DIM, 1)),
            jnp.where(first_head, pltpu.roll(head[2], HEAD_DIM, 1), head[3]),
        ],
        axis=1,
    ).astype(bfloat16)
    part[...] = dot(attended, out_ref[...]).astype(bfloat16)

    mix_copies = []
    for step in range(1, LANES):
        other = lax.rem(me + step, LANES)
        mix_copies.append(
            send(
                part.at[pl.ds(pl.multiple_of(other * rows, rows), rows)],
                part_held.at[step - 1],
                mix_send.at[step - 1],
                mix_recv.at[step - 1],
                (req, other),
            )
        )
    for copy in mix_copies:
        copy.start()
    for copy in near_weights():
        copy.wait()
    for copy in far_weights():
        copy.start()
    total = part[own_place, :].astype(float32)
    for step, copy in enumerate(mix_copies):
        copy.wait()
        total = total + part_held[step].astype(float32)
    mixed = (own_ref[...].astype(float32) + total).astype(bfloat16)
    expert_in = rms_scale(mixed, expert_gain_ref[...]).astype(bfloat16)

    expert_at = iota((rows, EXPERTS), 1)
    named = jnp.zeros((rows, EXPERTS), float32)
    for choice in range(TOPK):
        named = named + jnp.where(routes_ref[:, choice : choice + 1] == expert_at, 1.0, 0.0)
    gate_expo = jnp.where(named > 0.0, jnp.exp(dot(expert_in, router_ref[...])), 0.0)
    gate_values = (gate_expo / jnp.sum(gate_expo, axis=-1, keepdims=True)).astype(bfloat16)
    earlier = one_hot(iota((rows, rows), 1) < iota((rows, rows), 0))
    ranks = jnp.where(named > 0.0, dot(earlier, named.astype(bfloat16)), 99.0).astype(bfloat16)
    slots = EXPERTS * SLOT_ROWS
    spread = one_hot(iota((slots, EXPERTS), 0) // SLOT_ROWS == iota((slots, EXPERTS), 1))
    slot_rank = dot_last(spread, ranks)
    slot_row = lax.rem(iota((slots, rows), 0), SLOT_ROWS)
    chunks = PACKED // CHUNK

    def picker(chunk):
        return one_hot(slot_rank == packed_rank(slot_row, chunk).astype(float32))

    main = picker(None)
    for chunk in range(chunks):
        span = slice(chunk * CHUNK, (chunk + 1) * CHUNK)
        piece = dot(main, expert_in[:, span]) + dot(picker(chunk), expert_in[:, PACKED:])
        outgoing[:, :, span] = piece.astype(bfloat16).reshape(EXPERTS, SLOT_ROWS, CHUNK)

    def target(step):
        far, near = step // 4, lax.rem(step, 4)
        to_z = lax.rem(z + far, RING_Z)
        sign = 1 - 2 * lax.rem(y + near, 2)
        to_y = lax.rem(y + sign * near + RING_Y, RING_Y)
        return to_z * RING_Y + to_y

    def origin(step):
        far, near = step // 4, lax.rem(step, 4)
        from_z = lax.rem(z - far + RING_Z, RING_Z)
        sign = 1 - 2 * lax.rem(y, 2)
        from_y = lax.rem(y - sign * near + RING_Y, RING_Y)
        return from_z * RING_Y + from_y

    def go_copy(step):
        to = target(step)
        return send(
            outgoing.at[to // 2], arrived.at[step], go_send.at[step], go_recv.at[step], (to * 2 + core, me)
        )

    def return_copy(step):
        return send(
            result.at[step],
            back.at[mine],
            ret_send.at[step],
            ret_recv.at[step],
            (origin(step) * 2 + core, me),
        )

    own_block = pltpu.make_async_copy(outgoing.at[mine], arrived.at[0], local_sem.at[1])
    own_block.start()

    @pl.loop(1, experts)
    def _(step):
        go_copy(step).start()

    own_block.wait()
    for copy in far_weights():
        copy.wait()

    group = 8
    group_rows = group * SLOT_ROWS
    row_at, column_at = iota((group_rows, group_rows), 0), iota((group_rows, group_rows), 1)
    same_slot = row_at // SLOT_ROWS == column_at // SLOT_ROWS
    row_in, column_in = lax.rem(row_at, SLOT_ROWS), lax.rem(column_at, SLOT_ROWS)
    kept = one_hot(same_slot & (packed_rank(row_in, None) == column_in))
    packs = [one_hot(same_slot & (packed_rank(row_in, chunk) == column_in)) for chunk in range(chunks)]
    unpacks = [one_hot(same_slot & (packed_rank(column_in, chunk) == row_in)) for chunk in range(chunks)]

    @pl.loop(0, experts // group)
    def _(number):
        first = number * group
        for offset in range(group):
            step = first + offset

            @pl.when(step > 0)
            def _():
                go_copy(step).wait_recv()

        block = arrived[pl.ds(first, group)].reshape(group_rows, PACKED)
        end = None
        for chunk in range(chunks):
            moved = dot(unpacks[chunk], block[:, chunk * CHUNK : (chunk + 1) * CHUNK])
            end = moved if end is None else end + moved
        whole = jnp.concatenate([block, end.astype(bfloat16)], axis=1)
        total = None
        for held in range(LANES):
            gate_block = gate_ref[...] if held == 0 else gates[held - 1]
            up_block = up_ref[...] if held == 0 else ups[held - 1]
            down_block = down_ref[...] if held == 0 else downs[held - 1]
            gate_part = dot(whole, gate_block)
            up_part = dot(whole, up_block)
            hidden = (gate_part / (1.0 + jnp.exp(-gate_part)) * up_part).astype(bfloat16)
            term = dot(hidden, down_block)
            total = term if total is None else total + term
        rounded = total.astype(bfloat16)
        for chunk in range(chunks):
            span = slice(chunk * CHUNK, (chunk + 1) * CHUNK)
            piece = dot(kept, rounded[:, span]) + dot(packs[chunk], rounded[:, PACKED:])
            result[pl.ds(first, group), :, span] = piece.astype(bfloat16).reshape(
                group, SLOT_ROWS, CHUNK
            )
        for offset in range(group):
            step = first + offset

            @pl.when(step > 0)
            def _():
                return_copy(step).start()

    own_back = pltpu.make_async_copy(result.at[0], back.at[mine], local_sem.at[2])
    own_back.start()
    wide_spread = one_hot(iota((EXPERTS, slots), 1) // SLOT_ROWS == iota((EXPERTS, slots), 0))
    row_rank = dot(ranks, wide_spread)
    row_gate = dot(gate_values, wide_spread)
    slot_column = lax.rem(iota((rows, slots), 1), SLOT_ROWS)

    def combine(chunk):
        found = row_rank == packed_rank(slot_column, chunk).astype(float32)
        return jnp.where(found, row_gate, 0.0).astype(bfloat16)

    main = combine(None)
    ends = [combine(chunk) for chunk in range(chunks)]
    own_back.wait()

    @pl.loop(1, experts)
    def _(step):
        return_copy(step).wait_recv()

    end = None
    sums = []
    for chunk in range(chunks):
        piece = back[:, :, chunk * CHUNK : (chunk + 1) * CHUNK].reshape(slots, CHUNK)
        sums.append(dot(main, piece))
        moved = dot(ends[chunk], piece)
        end = moved if end is None else end + moved
    sums.append(end)
    layer = (mixed.astype(float32) + jnp.concatenate(sums, axis=1)).astype(bfloat16)
    layer_ref[...] = layer
    parts = width // 128
    closing = layer[rows - 8 :, :].astype(float32)
    tail[...] = jnp.concatenate(
        [closing[7:8, at * 128 : (at + 1) * 128] for at in range(parts)], axis=0
    ).astype(bfloat16)

    def lane_copy(to):
        return send(tail, tails.at[core, place], lane_send.at[to], lane_recv, (req, to))

    @pl.when(me == last)
    def _():
        for to in range(last):
            lane_copy(to).start()
        own = pltpu.make_async_copy(tail, tails.at[core, place], local_sem.at[3])
        own.start()
        own.wait()
        for to in range(last):
            lane_copy(to).wait_send()

    @pl.when(me != last)
    def _():
        send(tail, tails.at[core, place], lane_send.at[0], lane_recv, (req, last)).wait_recv()

    def plane_copy(step):
        own_row = tails.at[core, place]
        return send(own_row, own_row, plane_send.at[step], plane_recv.at[step], plane_peer(step))

    @pl.loop(1, places)
    def _(step):
        plane_copy(step).start()

    @pl.loop(1, experts)
    def _(step):
        go_copy(step).wait_send()
        return_copy(step).wait_send()

    @pl.loop(1, places)
    def _(step):
        plane_copy(step).wait()

    half = send(tails.at[core], tails.at[core], core_sem.at[0], core_sem.at[1], (partner, me))
    half.start()
    half.wait()

    count = 2 * places
    tails_wide[...] = tails[...].astype(float32).reshape(count, parts, 128)
    square = jnp.zeros((count, 1), float32)
    for at in range(parts):
        piece = tails_wide[:, at, :]
        square = square + jnp.sum(piece * piece, axis=-1, keepdims=True)
    scale = lax.rsqrt(square / width + epsilon)
    chosen = one_hot(iota((count, count), 0) == order_ref[...])
    found = jnp.zeros(logits_ref.shape, float32)
    for at in range(parts):
        span = slice(at * 128, (at + 1) * 128)
        final = (tails_wide[:, at, :] * scale * final_gain_ref[:, span]).astype(bfloat16)
        ordered = dot(chosen, final).astype(bfloat16)
        found = found + dot(ordered, vocab_ref[span, :])
    logits_ref[...] = found


def body(
    hidden_in,
    cache_keys,
    cache_values,
    lengths,
    request_order,
    routes,
    query_weight,
    key_weight,
    value_weight,
    out_weight,
    attention_gain,
    expert_gain,
    router_weight,
    gate_weight,
    up_weight,
    down_weight,
    final_gain,
    vocab_weight,
):
    own_rows = hidden_in[0]
    rows, width = own_rows.shape
    units = gate_weight.shape[2]
    reqs = lengths.shape[0]
    places = reqs // 2
    half_dim = HEAD_DIM // 2
    frequency = jnp.exp(
        -jnp.log(10000.0) * jnp.arange(half_dim, dtype=float32) * (2.0 / HEAD_DIM)
    )
    positions = lengths[lax.axis_index("req")] + jnp.arange(SPAN, dtype=jnp.int32)
    angles = positions.astype(float32)[:, None] * jnp.tile(frequency, 128 // half_dim)[None, :]
    table = jnp.stack([jnp.cos(angles), jnp.sin(angles)])
    lane_routes = lax.dynamic_slice_in_dim(routes[0], lax.axis_index("tp") * rows, rows, 0)
    order = request_order.reshape(places, 2).T.reshape(1, reqs)
    dma = pltpu.SemaphoreType.DMA
    heads = 4 * SPAN
    slot_block = pltpu.VMEM((EXPERTS, SLOT_ROWS, PACKED), bfloat16)
    layer_rows, logits = pl.pallas_call(
        layer_kernel,
        out_shape=[
            jax.ShapeDtypeStruct((rows, width), bfloat16),
            jax.ShapeDtypeStruct((reqs, vocab_weight.shape[1]), float32),
        ],
        in_specs=[pl.BlockSpec(memory_space=pltpu.SMEM)] + [VMEM_SPEC] * 18,
        out_specs=[VMEM_SPEC] * 2,
        scratch_shapes=[
            pltpu.VMEM((rows, width), bfloat16),
            pltpu.VMEM((SPAN, width), bfloat16),
            pltpu.VMEM((heads, 128), bfloat16),
            pltpu.VMEM((heads, 128), float32),
            pltpu.VMEM((heads, 1), float32),
            pltpu.VMEM((SPAN, width), bfloat16),
            pltpu.VMEM((LANES - 1, rows, width), bfloat16),
            slot_block,
            slot_block,
            slot_block,
            slot_block,
            pltpu.VMEM((LANES - 1, width, units), bfloat16),
            pltpu.VMEM((LANES - 1, width, units), bfloat16),
            pltpu.VMEM((LANES - 1, units, width), bfloat16),
            pltpu.VMEM((width // 128, 128), bfloat16),
            pltpu.VMEM((2, places, width // 128, 128), bfloat16),
            pltpu.VMEM((reqs, width // 128, 128), float32),
            dma((LANES - 1,)),
            dma((LANES - 1,)),
            dma((LANES - 1,)),
            dma((LANES - 1,)),
            dma((4, 3)),
            dma((4, 3)),
            dma((EXPERTS,)),
            dma((EXPERTS,)),
            dma((EXPERTS,)),
            dma((EXPERTS,)),
            dma((LANES - 1,)),
            dma,
            dma((places,)),
            dma((places,)),
            dma((2,)),
            dma((4,)),
        ],
        compiler_params=pltpu.CompilerParams(
            collective_id=0, has_side_effects=True, vmem_limit_bytes=48 * 1024 * 1024
        ),
        name="layer",
    )(
        lengths,
        own_rows,
        cache_keys[0],
        cache_values[0],
        table,
        lane_routes,
        query_weight,
        key_weight,
        value_weight,
        out_weight,
        attention_gain.reshape(1, width),
        expert_gain.reshape(1, width),
        router_weight,
        gate_weight[0],
        up_weight[0],
        down_weight[0],
        final_gain.reshape(1, width),
        order,
        vocab_weight,
    )
    return (layer_rows[None], logits)


def solution(mesh):
    in_specs = (
        P("req", "tp", None),
        P("req", None, "tp"),
        P("req", None, "tp"),
        P(),
        P(),
        P("req", None, None),
        P(None, "tp"),
        P(None, "tp"),
        P(None, "tp"),
        P("tp", None),
        P(),
        P(),
        P(),
        P("req", None, "tp"),
        P("req", None, "tp"),
        P("req", "tp", None),
        P(),
        P(None, ("req", "tp")),
    )
    out_specs = (P("req", "tp", None), P(None, ("req", "tp")))
    return jax.shard_map(body, mesh=mesh, in_specs=in_specs, out_specs=out_specs, check_vma=False)
```

```python
import jax
import jax.numpy as jnp
import numpy as np
from jax.experimental import pallas as pl
from jax.experimental.pallas import tpu as pltpu
from jax import lax
from jax.sharding import PartitionSpec as P

HEAD_DIM = 64
EXPERTS = 32
TOPK = 8
LANES = 4
RING_Y = 8
RING_Z = 8
SPAN = 128
SLOT_ROWS = 16
CAP = 12
PACKED = 768
CHUNK = 256
MESH = pl.DeviceIdType.MESH
VMEM_SPEC = pl.BlockSpec(memory_space=pltpu.VMEM)


epsilon = 1e-06
key_block = 512
float32 = jnp.float32
bfloat16 = jnp.bfloat16


def rms_scale(row_block, gain_vector):
    widened = row_block.astype(jnp.float32)
    return (
        widened
        * lax.rsqrt(jnp.mean(widened * widened, axis=-1, keepdims=True) + epsilon)
        * gain_vector
    )


def send(source, target, send_sem, recv_sem, device):
    return pltpu.make_async_remote_copy(
        src_ref=source,
        dst_ref=target,
        send_sem=send_sem,
        recv_sem=recv_sem,
        device_id=device,
        device_id_type=MESH,
    )


def greet(barrier, device):
    pl.semaphore_signal(barrier, inc=1, device_id=device, device_id_type=MESH)


def dot(a, b):
    return jnp.dot(a, b, preferred_element_type=float32)


def dot_last(a, b):
    return lax.dot_general(a, b, (((1,), (1,)), ((), ())), preferred_element_type=float32)


def iota(shape, axis):
    return lax.broadcasted_iota(jnp.int32, shape, axis)


def one_hot(mask):
    return jnp.where(mask, 1.0, 0.0).astype(bfloat16)


def packed_rank(slot_row, chunk):
    if chunk is None:
        return jnp.where(slot_row < CAP, slot_row, -1)
    return jnp.where(slot_row >= CAP, slot_row - CAP + (SLOT_ROWS - CAP) * chunk, -1)


def layer_kernel(
    frequency_ref,
    length_hbm,
    own_hbm,
    keys_hbm,
    values_hbm,
    routes_hbm,
    query_hbm,
    key_hbm,
    value_hbm,
    out_hbm,
    attention_gain_hbm,
    expert_gain_hbm,
    router_hbm,
    gate_hbm,
    up_hbm,
    down_hbm,
    final_gain_hbm,
    order_hbm,
    vocab_hbm,
    layer_ref,
    logits_ref,
    length_ref,
    own_ref,
    keys_ref,
    values_ref,
    routes_ref,
    query_ref,
    key_ref,
    value_ref,
    out_ref,
    attention_gain_ref,
    expert_gain_ref,
    router_ref,
    gate_ref,
    up_ref,
    down_ref,
    final_gain_ref,
    order_ref,
    vocab_ref,
    normed,
    all_rows,
    stacked,
    numerator,
    denominator,
    part,
    part_held,
    outgoing,
    arrived,
    result,
    back,
    gates,
    ups,
    downs,
    tail,
    tails,
    tails_wide,
    row_send,
    row_recv,
    mix_send,
    mix_recv,
    weight_send,
    weight_recv,
    go_send,
    go_recv,
    ret_send,
    ret_recv,
    lane_send,
    lane_recv,
    plane_send,
    plane_recv,
    core_sem,
    local_sem,
    load_sem,
):
    req, me = lax.axis_index("req"), lax.axis_index("tp")
    z, y, core = req // (2 * RING_Y), lax.rem(req // 2, RING_Y), lax.rem(req, 2)
    place = req // 2
    places = RING_Y * RING_Z
    mine = place // 2
    experts, _, _ = outgoing.shape
    rows, width = own_ref.shape
    partner = z * 2 * RING_Y + y * 2 + 1 - core
    last = LANES - 1
    barrier = pltpu.get_barrier_semaphore()

    def lane(step):
        return (req, lax.rem(me + step, LANES))

    def plane_peer(step):
        return (lax.rem(place + step, places) * 2 + core, me)

    for step in range(1, LANES):
        greet(barrier, lane(step))
    greet(barrier, (partner, me))

    @pl.loop(1, places)
    def _(step):
        greet(barrier, plane_peer(step))

    loads = {}
    for number, (name, source, held) in enumerate(
        (
            ("own", own_hbm, own_ref),
            ("attention_gain", attention_gain_hbm, attention_gain_ref),
            ("length", length_hbm, length_ref),
            ("keys", keys_hbm, keys_ref),
            ("values", values_hbm, values_ref),
            ("routes", routes_hbm, routes_ref),
            ("query", query_hbm, query_ref),
            ("key", key_hbm, key_ref),
            ("value", value_hbm, value_ref),
            ("out", out_hbm, out_ref),
            ("expert_gain", expert_gain_hbm, expert_gain_ref),
            ("router", router_hbm, router_ref),
            ("gate", gate_hbm, gate_ref),
            ("up", up_hbm, up_ref),
            ("down", down_hbm, down_ref),
            ("final_gain", final_gain_hbm, final_gain_ref),
            ("order", order_hbm, order_ref),
            ("vocab", vocab_hbm, vocab_ref),
        )
    ):
        loads[name] = pltpu.make_async_copy(source, held, load_sem.at[number])
        loads[name].start()

    def ready(*wanted):
        for name in wanted:
            loads[name].wait()

    ready("own", "attention_gain", "length")
    normed[...] = rms_scale(own_ref[...], attention_gain_ref[...]).astype(bfloat16)
    own_place = pl.ds(pl.multiple_of(me * rows, rows), rows)
    local = pltpu.make_async_copy(normed, all_rows.at[own_place], local_sem.at[0])
    local.start()
    length = length_ref[req]
    positions = (length + iota((SPAN, 128), 0)).astype(float32)
    angles = positions * frequency_ref[...]
    cosine, sine = jnp.cos(angles), jnp.sin(angles)
    pl.semaphore_wait(barrier, LANES - 1 + 1 + places - 1)

    row_copies = [
        send(normed, all_rows.at[own_place], row_send.at[step - 1], row_recv.at[step - 1], lane(step))
        for step in range(1, LANES)
    ]
    for copy in row_copies:
        copy.start()
    triples = ((gate_hbm, gates), (up_hbm, ups), (down_hbm, downs))

    def near_weights():
        return [
            send(
                source,
                target.at[side],
                weight_send.at[side, number],
                weight_recv.at[side, number],
                lane((1, LANES - 1)[side]),
            )
            for number, (source, target) in enumerate(triples)
            for side in range(2)
        ]

    def far_weights():
        found = []
        for number, (source, target) in enumerate(triples):
            half = source.shape[0] // 2
            for side in range(2):
                piece = pl.ds(side * half, half)
                found.append(
                    send(
                        target.at[side, piece],
                        target.at[2, piece],
                        weight_send.at[2 + side, number],
                        weight_recv.at[2 + side, number],
                        lane((1, LANES - 1)[side]),
                    )
                )
        return found

    for copy in near_weights():
        copy.start()
    for copy in row_copies:
        copy.wait()
    local.wait()

    lanes_at = iota((SPAN, 128), 1)
    front = lax.rem(lanes_at, HEAD_DIM) < HEAD_DIM // 2
    first_head = lanes_at < HEAD_DIM
    token_rows = all_rows[...]

    def turned(piece):
        other = jnp.where(
            front, -pltpu.roll(piece, 128 - HEAD_DIM // 2, 1), pltpu.roll(piece, HEAD_DIM // 2, 1)
        )
        return piece * cosine + other * sine

    ready("query", "key", "value")
    projected = dot(token_rows, query_ref[...])
    zero = jnp.zeros((SPAN, 128), float32)
    for group in range(2):
        piece = turned(projected[:, group * 128 : (group + 1) * 128]).astype(bfloat16).astype(float32)
        piece = piece * HEAD_DIM ** (-0.5)
        swapped = pltpu.roll(piece, HEAD_DIM, 1)
        keep = first_head if group == 0 else jnp.logical_not(first_head)
        pair = (piece, swapped) if group == 0 else (swapped, piece)
        for member in range(2):
            at = (group * 2 + member) * SPAN
            stacked[at : at + SPAN, :] = jnp.where(keep, pair[member], zero).astype(bfloat16)
    new_keys = turned(dot(token_rows, key_ref[...])).astype(bfloat16)
    new_values = dot(token_rows, value_ref[...]).astype(bfloat16)
    heads = 4 * SPAN
    causal = iota((heads, SPAN), 1) <= lax.rem(iota((heads, SPAN), 0), SPAN)
    expo = jnp.where(causal, jnp.exp(dot_last(stacked[...], new_keys)), 0.0)
    numerator[...] = dot(expo.astype(bfloat16), new_values)
    denominator[...] = jnp.sum(expo, axis=-1, keepdims=True)
    ready("keys", "values")

    @pl.loop(0, keys_ref.shape[0] // key_block)
    def _(number):
        at = pl.ds(pl.multiple_of(number * key_block, key_block), key_block)
        scores = dot_last(stacked[...], keys_ref[at, :])
        inside = iota((heads, key_block), 1) < length - number * key_block
        block = jnp.where(inside, jnp.exp(scores), 0.0)
        numerator[...] += dot(block.astype(bfloat16), values_ref[at, :])
        denominator[...] += jnp.sum(block, axis=-1, keepdims=True)

    ready("out")
    mean_values = numerator[...] / denominator[...]
    head = [mean_values[at * SPAN : (at + 1) * SPAN] for at in range(4)]
    attended = jnp.concatenate(
        [
            jnp.where(first_head, head[0], pltpu.roll(head[1], HEAD_DIM, 1)),
            jnp.where(first_head, pltpu.roll(head[2], HEAD_DIM, 1), head[3]),
        ],
        axis=1,
    ).astype(bfloat16)
    part[...] = dot(attended, out_ref[...]).astype(bfloat16)

    mix_copies = []
    for step in range(1, LANES):
        other = lax.rem(me + step, LANES)
        mix_copies.append(
            send(
                part.at[pl.ds(pl.multiple_of(other * rows, rows), rows)],
                part_held.at[step - 1],
                mix_send.at[step - 1],
                mix_recv.at[step - 1],
                (req, other),
            )
        )
    for copy in mix_copies:
        copy.start()
    for copy in near_weights():
        copy.wait()
    for copy in far_weights():
        copy.start()
    total = part[own_place, :].astype(float32)
    for step, copy in enumerate(mix_copies):
        copy.wait()
        total = total + part_held[step].astype(float32)
    ready("expert_gain", "router", "routes")
    mixed = (own_ref[...].astype(float32) + total).astype(bfloat16)
    expert_in = rms_scale(mixed, expert_gain_ref[...]).astype(bfloat16)

    expert_at = iota((EXPERTS, SPAN), 0)
    every_named = jnp.zeros((EXPERTS, SPAN), float32)
    for choice in range(TOPK):
        every_named = every_named + jnp.where(routes_ref[choice : choice + 1, :] == expert_at, 1.0, 0.0)
    own_tokens = one_hot(iota((rows, SPAN), 1) == iota((rows, SPAN), 0) + me * rows)
    named = dot_last(own_tokens, every_named.astype(bfloat16))
    gate_expo = jnp.where(named > 0.0, jnp.exp(dot_last(expert_in, router_ref[...])), 0.0)
    gate_values = (gate_expo / jnp.sum(gate_expo, axis=-1, keepdims=True)).astype(bfloat16)
    earlier = one_hot(iota((rows, rows), 1) < iota((rows, rows), 0))
    ranks = jnp.where(named > 0.0, dot(earlier, named.astype(bfloat16)), 99.0).astype(bfloat16)
    slots = EXPERTS * SLOT_ROWS
    spread = one_hot(iota((slots, EXPERTS), 0) // SLOT_ROWS == iota((slots, EXPERTS), 1))
    slot_rank = dot_last(spread, ranks)
    slot_row = lax.rem(iota((slots, rows), 0), SLOT_ROWS)
    chunks = PACKED // CHUNK

    def picker(chunk):
        return one_hot(slot_rank == packed_rank(slot_row, chunk).astype(float32))

    main = picker(None)
    for chunk in range(chunks):
        span = slice(chunk * CHUNK, (chunk + 1) * CHUNK)
        piece = dot(main, expert_in[:, span]) + dot(picker(chunk), expert_in[:, PACKED:])
        outgoing[:, :, span] = piece.astype(bfloat16).reshape(EXPERTS, SLOT_ROWS, CHUNK)

    def target(step):
        far, near = step // 4, lax.rem(step, 4)
        to_z = lax.rem(z + far, RING_Z)
        sign = 1 - 2 * lax.rem(y + near, 2)
        to_y = lax.rem(y + sign * near + RING_Y, RING_Y)
        return to_z * RING_Y + to_y

    def origin(step):
        far, near = step // 4, lax.rem(step, 4)
        from_z = lax.rem(z - far + RING_Z, RING_Z)
        sign = 1 - 2 * lax.rem(y, 2)
        from_y = lax.rem(y - sign * near + RING_Y, RING_Y)
        return from_z * RING_Y + from_y

    def go_copy(step):
        to = target(step)
        return send(
            outgoing.at[to // 2], arrived.at[step], go_send.at[step], go_recv.at[step], (to * 2 + core, me)
        )

    def return_copy(step):
        return send(
            result.at[step],
            back.at[mine],
            ret_send.at[step],
            ret_recv.at[step],
            (origin(step) * 2 + core, me),
        )

    own_block = pltpu.make_async_copy(outgoing.at[mine], arrived.at[0], local_sem.at[1])
    own_block.start()

    @pl.loop(1, experts)
    def _(step):
        go_copy(step).start()

    own_block.wait()
    for copy in far_weights():
        copy.wait()

    ready("gate", "up", "down")
    group = 8
    group_rows = group * SLOT_ROWS
    row_at, column_at = iota((group_rows, group_rows), 0), iota((group_rows, group_rows), 1)
    same_slot = row_at // SLOT_ROWS == column_at // SLOT_ROWS
    row_in, column_in = lax.rem(row_at, SLOT_ROWS), lax.rem(column_at, SLOT_ROWS)
    kept = one_hot(same_slot & (packed_rank(row_in, None) == column_in))
    packs = [one_hot(same_slot & (packed_rank(row_in, chunk) == column_in)) for chunk in range(chunks)]
    unpacks = [one_hot(same_slot & (packed_rank(column_in, chunk) == row_in)) for chunk in range(chunks)]

    @pl.loop(0, experts // group)
    def _(number):
        first = number * group
        for offset in range(group):
            step = first + offset

            @pl.when(step > 0)
            def _():
                go_copy(step).wait_recv()

        block = arrived[pl.ds(first, group)].reshape(group_rows, PACKED)
        end = None
        for chunk in range(chunks):
            moved = dot(unpacks[chunk], block[:, chunk * CHUNK : (chunk + 1) * CHUNK])
            end = moved if end is None else end + moved
        whole = jnp.concatenate([block, end.astype(bfloat16)], axis=1)
        total = None
        for held in range(LANES):
            gate_block = gate_ref[...] if held == 0 else gates[held - 1]
            up_block = up_ref[...] if held == 0 else ups[held - 1]
            down_block = down_ref[...] if held == 0 else downs[held - 1]
            gate_part = dot(whole, gate_block)
            up_part = dot(whole, up_block)
            hidden = (gate_part / (1.0 + jnp.exp(-gate_part)) * up_part).astype(bfloat16)
            term = dot(hidden, down_block)
            total = term if total is None else total + term
        rounded = total.astype(bfloat16)
        for chunk in range(chunks):
            span = slice(chunk * CHUNK, (chunk + 1) * CHUNK)
            piece = dot(kept, rounded[:, span]) + dot(packs[chunk], rounded[:, PACKED:])
            result[pl.ds(first, group), :, span] = piece.astype(bfloat16).reshape(
                group, SLOT_ROWS, CHUNK
            )
        for offset in range(group):
            step = first + offset

            @pl.when(step > 0)
            def _():
                return_copy(step).start()

    own_back = pltpu.make_async_copy(result.at[0], back.at[mine], local_sem.at[2])
    own_back.start()
    wide_spread = one_hot(iota((EXPERTS, slots), 1) // SLOT_ROWS == iota((EXPERTS, slots), 0))
    row_rank = dot(ranks, wide_spread)
    row_gate = dot(gate_values, wide_spread)
    slot_column = lax.rem(iota((rows, slots), 1), SLOT_ROWS)

    def combine(chunk):
        found = row_rank == packed_rank(slot_column, chunk).astype(float32)
        return jnp.where(found, row_gate, 0.0).astype(bfloat16)

    main = combine(None)
    ends = [combine(chunk) for chunk in range(chunks)]
    own_back.wait()

    @pl.loop(1, experts)
    def _(step):
        return_copy(step).wait_recv()

    end = None
    sums = []
    for chunk in range(chunks):
        piece = back[:, :, chunk * CHUNK : (chunk + 1) * CHUNK].reshape(slots, CHUNK)
        sums.append(dot(main, piece))
        moved = dot(ends[chunk], piece)
        end = moved if end is None else end + moved
    sums.append(end)
    layer = (mixed.astype(float32) + jnp.concatenate(sums, axis=1)).astype(bfloat16)
    layer_ref[...] = layer
    parts = width // 128
    closing = layer[rows - 8 :, :].astype(float32)
    tail[...] = jnp.concatenate(
        [closing[7:8, at * 128 : (at + 1) * 128] for at in range(parts)], axis=0
    ).astype(bfloat16)

    def lane_copy(to):
        return send(tail, tails.at[core, place], lane_send.at[to], lane_recv, (req, to))

    @pl.when(me == last)
    def _():
        for to in range(last):
            lane_copy(to).start()
        own = pltpu.make_async_copy(tail, tails.at[core, place], local_sem.at[3])
        own.start()
        own.wait()
        for to in range(last):
            lane_copy(to).wait_send()

    @pl.when(me != last)
    def _():
        send(tail, tails.at[core, place], lane_send.at[0], lane_recv, (req, last)).wait_recv()

    def plane_copy(step):
        own_row = tails.at[core, place]
        return send(own_row, own_row, plane_send.at[step], plane_recv.at[step], plane_peer(step))

    @pl.loop(1, places)
    def _(step):
        plane_copy(step).start()

    @pl.loop(1, experts)
    def _(step):
        go_copy(step).wait_send()
        return_copy(step).wait_send()

    @pl.loop(1, places)
    def _(step):
        plane_copy(step).wait()

    half = send(tails.at[core], tails.at[core], core_sem.at[0], core_sem.at[1], (partner, me))
    half.start()
    half.wait()

    ready("final_gain", "order", "vocab")
    count = 2 * places
    tails_wide[...] = tails[...].astype(float32).reshape(count, parts, 128)
    square = jnp.zeros((count, 1), float32)
    for at in range(parts):
        piece = tails_wide[:, at, :]
        square = square + jnp.sum(piece * piece, axis=-1, keepdims=True)
    scale = lax.rsqrt(square / width + epsilon)
    by_slot = one_hot(iota((count, count), 0) == order_ref[...])
    slot_at, held_at = iota((count, count), 0), iota((count, count), 1)
    held_slot = lax.rem(held_at, places) * 2 + held_at // places
    chosen = dot(by_slot, one_hot(slot_at == held_slot)).astype(bfloat16)
    found = jnp.zeros(logits_ref.shape, float32)
    for at in range(parts):
        span = slice(at * 128, (at + 1) * 128)
        final = (tails_wide[:, at, :] * scale * final_gain_ref[:, span]).astype(bfloat16)
        ordered = dot(chosen, final).astype(bfloat16)
        found = found + dot_last(vocab_ref[:, span], ordered)
    logits_ref[...] = found


def body(
    hidden_in,
    cache_keys,
    cache_values,
    lengths,
    request_order,
    routes,
    query_weight,
    key_weight,
    value_weight,
    out_weight,
    attention_gain,
    expert_gain,
    router_weight,
    gate_weight,
    up_weight,
    down_weight,
    final_gain,
    vocab_weight,
):
    own_rows = hidden_in[0]
    rows, width = own_rows.shape
    units = gate_weight.shape[2]
    reqs = lengths.shape[0]
    places = reqs // 2
    half_dim = HEAD_DIM // 2
    frequency = np.exp(-np.log(10000.0) * np.arange(half_dim) * (2.0 / HEAD_DIM)).astype(np.float32)
    frequency = jnp.asarray(np.tile(frequency, 128 // half_dim)[None, :])
    operands = [
        lengths,
        own_rows,
        cache_keys[0],
        cache_values[0],
        routes[0].T,
        query_weight,
        key_weight,
        value_weight,
        out_weight,
        attention_gain.reshape(1, width),
        expert_gain.reshape(1, width),
        router_weight.T,
        gate_weight[0],
        up_weight[0],
        down_weight[0],
        final_gain.reshape(1, width),
        request_order.reshape(1, reqs),
        vocab_weight.T,
    ]
    dma = pltpu.SemaphoreType.DMA
    heads = 4 * SPAN
    slot_block = pltpu.VMEM((EXPERTS, SLOT_ROWS, PACKED), bfloat16)
    layer_rows, logits = pl.pallas_call(
        layer_kernel,
        out_shape=[
            jax.ShapeDtypeStruct((rows, width), bfloat16),
            jax.ShapeDtypeStruct((vocab_weight.shape[1], reqs), float32),
        ],
        in_specs=[VMEM_SPEC] + [pl.BlockSpec(memory_space=pltpu.HBM)] * len(operands),
        out_specs=[VMEM_SPEC] * 2,
        scratch_shapes=[pltpu.SMEM((reqs,), jnp.int32)]
        + [pltpu.VMEM(operand.shape, operand.dtype) for operand in operands[1:]]
        + [
            pltpu.VMEM((rows, width), bfloat16),
            pltpu.VMEM((SPAN, width), bfloat16),
            pltpu.VMEM((heads, 128), bfloat16),
            pltpu.VMEM((heads, 128), float32),
            pltpu.VMEM((heads, 1), float32),
            pltpu.VMEM((SPAN, width), bfloat16),
            pltpu.VMEM((LANES - 1, rows, width), bfloat16),
            slot_block,
            slot_block,
            slot_block,
            slot_block,
            pltpu.VMEM((LANES - 1, width, units), bfloat16),
            pltpu.VMEM((LANES - 1, width, units), bfloat16),
            pltpu.VMEM((LANES - 1, units, width), bfloat16),
            pltpu.VMEM((width // 128, 128), bfloat16),
            pltpu.VMEM((2, places, width // 128, 128), bfloat16),
            pltpu.VMEM((reqs, width // 128, 128), float32),
            dma((LANES - 1,)),
            dma((LANES - 1,)),
            dma((LANES - 1,)),
            dma((LANES - 1,)),
            dma((4, 3)),
            dma((4, 3)),
            dma((EXPERTS,)),
            dma((EXPERTS,)),
            dma((EXPERTS,)),
            dma((EXPERTS,)),
            dma((LANES - 1,)),
            dma,
            dma((places,)),
            dma((places,)),
            dma((2,)),
            dma((4,)),
            dma((len(operands),)),
        ],
        compiler_params=pltpu.CompilerParams(
            collective_id=0, has_side_effects=True, vmem_limit_bytes=67043328
        ),
        name="layer",
    )(frequency, *operands)
    return (layer_rows[None], logits.T)


def solution(mesh):
    in_specs = (
        P("req", "tp", None),
        P("req", None, "tp"),
        P("req", None, "tp"),
        P(),
        P(),
        P("req", None, None),
        P(None, "tp"),
        P(None, "tp"),
        P(None, "tp"),
        P("tp", None),
        P(),
        P(),
        P(),
        P("req", None, "tp"),
        P("req", None, "tp"),
        P("req", "tp", None),
        P(),
        P(None, ("req", "tp")),
    )
    out_specs = (P("req", "tp", None), P(None, ("req", "tp")))
    return jax.shard_map(body, mesh=mesh, in_specs=in_specs, out_specs=out_specs, check_vma=False)
```

```python
import jax
import jax.numpy as jnp
import numpy as np
from jax.experimental import pallas as pl
from jax.experimental.pallas import tpu as pltpu
from jax import lax
from jax.sharding import PartitionSpec as P

HEAD_DIM = 64
EXPERTS = 32
TOPK = 8
LANES = 4
RING_Y = 8
RING_Z = 8
SPAN = 128
SLOT_ROWS = 16
CAP = 12
PACKED = 768
CHUNK = 256
MESH = pl.DeviceIdType.MESH
VMEM_SPEC = pl.BlockSpec(memory_space=pltpu.VMEM)


epsilon = 1e-06
key_block = 512
float32 = jnp.float32
bfloat16 = jnp.bfloat16


def rms_scale(row_block, gain_vector):
    widened = row_block.astype(jnp.float32)
    return (
        widened
        * lax.rsqrt(jnp.mean(widened * widened, axis=-1, keepdims=True) + epsilon)
        * gain_vector
    )


def send(source, target, send_sem, recv_sem, device):
    return pltpu.make_async_remote_copy(
        src_ref=source,
        dst_ref=target,
        send_sem=send_sem,
        recv_sem=recv_sem,
        device_id=device,
        device_id_type=MESH,
    )


def greet(barrier, device):
    pl.semaphore_signal(barrier, inc=1, device_id=device, device_id_type=MESH)


def dot(a, b):
    return jnp.dot(a, b, preferred_element_type=float32)


def dot_last(a, b):
    return lax.dot_general(a, b, (((1,), (1,)), ((), ())), preferred_element_type=float32)


def iota(shape, axis):
    return lax.broadcasted_iota(jnp.int32, shape, axis)


def one_hot(mask):
    return jnp.where(mask, 1.0, 0.0).astype(bfloat16)


def packed_rank(slot_row, chunk):
    if chunk is None:
        return jnp.where(slot_row < CAP, slot_row, -1)
    return jnp.where(slot_row >= CAP, slot_row - CAP + (SLOT_ROWS - CAP) * chunk, -1)


def layer_kernel(
    frequency_ref,
    length_hbm,
    own_hbm,
    keys_hbm,
    values_hbm,
    routes_hbm,
    query_hbm,
    key_hbm,
    value_hbm,
    out_hbm,
    attention_gain_hbm,
    expert_gain_hbm,
    router_hbm,
    gate_hbm,
    up_hbm,
    down_hbm,
    final_gain_hbm,
    order_hbm,
    vocab_hbm,
    layer_ref,
    logits_ref,
    length_ref,
    own_ref,
    keys_ref,
    values_ref,
    routes_ref,
    query_ref,
    key_ref,
    value_ref,
    out_ref,
    attention_gain_ref,
    expert_gain_ref,
    router_ref,
    final_gain_ref,
    order_ref,
    vocab_ref,
    normed,
    all_rows,
    stacked,
    numerator,
    denominator,
    part,
    part_held,
    outgoing,
    arrived,
    result,
    back,
    entry,
    exit_rows,
    tail,
    tails,
    tails_wide,
    row_send,
    row_recv,
    mix_send,
    mix_recv,
    weight_send,
    weight_recv,
    go_send,
    go_recv,
    ret_send,
    ret_recv,
    lane_send,
    lane_recv,
    plane_send,
    plane_recv,
    core_sem,
    local_sem,
    load_sem,
):
    req, me = lax.axis_index("req"), lax.axis_index("tp")
    z, y, core = req // (2 * RING_Y), lax.rem(req // 2, RING_Y), lax.rem(req, 2)
    place = req // 2
    places = RING_Y * RING_Z
    mine = place // 2
    experts, _, _ = outgoing.shape
    rows, width = own_ref.shape
    units = down_hbm.shape[0]
    pair = 2 * units
    partner = z * 2 * RING_Y + y * 2 + 1 - core
    last = LANES - 1
    barrier = pltpu.get_barrier_semaphore()

    def lane(step):
        return (req, lax.rem(me + step, LANES))

    def plane_peer(step):
        return (lax.rem(place + step, places) * 2 + core, me)

    for step in range(1, LANES):
        greet(barrier, lane(step))
    greet(barrier, (partner, me))

    @pl.loop(1, places)
    def _(step):
        greet(barrier, plane_peer(step))

    loads = {}
    for number, (name, source, held) in enumerate(
        (
            ("own", own_hbm, own_ref),
            ("attention_gain", attention_gain_hbm, attention_gain_ref),
            ("length", length_hbm, length_ref),
            ("keys", keys_hbm, keys_ref),
            ("values", values_hbm, values_ref),
            ("routes", routes_hbm, routes_ref),
            ("query", query_hbm, query_ref),
            ("key", key_hbm, key_ref),
            ("value", value_hbm, value_ref),
            ("out", out_hbm, out_ref),
            ("expert_gain", expert_gain_hbm, expert_gain_ref),
            ("router", router_hbm, router_ref),
            ("gate", gate_hbm, entry.at[:, :units]),
            ("up", up_hbm, entry.at[:, units : 2 * units]),
            ("down", down_hbm, exit_rows.at[:units]),
            ("final_gain", final_gain_hbm, final_gain_ref),
            ("order", order_hbm, order_ref),
            ("vocab", vocab_hbm, vocab_ref),
        )
    ):
        loads[name] = pltpu.make_async_copy(source, held, load_sem.at[number])
        loads[name].start()

    def ready(*wanted):
        for name in wanted:
            loads[name].wait()

    ready("own", "attention_gain", "length")
    normed[...] = rms_scale(own_ref[...], attention_gain_ref[...]).astype(bfloat16)
    own_place = pl.ds(pl.multiple_of(me * rows, rows), rows)
    local = pltpu.make_async_copy(normed, all_rows.at[own_place], local_sem.at[0])
    local.start()
    length = length_ref[req]
    positions = (length + iota((SPAN, 128), 0)).astype(float32)
    angles = positions * frequency_ref[...]
    cosine, sine = jnp.cos(angles), jnp.sin(angles)
    pl.semaphore_wait(barrier, LANES - 1 + 1 + places - 1)

    row_copies = [
        send(normed, all_rows.at[own_place], row_send.at[step - 1], row_recv.at[step - 1], lane(step))
        for step in range(1, LANES)
    ]
    for copy in row_copies:
        copy.start()
    half = width // 2
    own_half = pl.ds(pl.multiple_of(core * half, half), half)

    def exit_at(slot, amount, side):
        first = slot * units + core * (units // 2) + side * amount
        return pl.ds(pl.multiple_of(first, amount), amount)

    def weight_copy(source, target, number, device):
        return send(source, target, weight_send.at[number], weight_recv.at[number], device)

    def near_weights():
        found = []
        for side in range(2):
            first = (1 + side) * pair
            to = lane((1, LANES - 1)[side])
            unit_half = pl.ds(pl.multiple_of(core * (units // 2), units // 2), units // 2)
            for number, (source, target) in enumerate(
                (
                    (gate_hbm.at[own_half], entry.at[own_half, first : first + units]),
                    (up_hbm.at[own_half], entry.at[own_half, first + units : first + pair]),
                    (down_hbm.at[unit_half], exit_rows.at[exit_at(1 + side, units // 2, 0)]),
                )
            ):
                found.append(weight_copy(source, target, side * 3 + number, to))
        return found

    def far_weights():
        found = []
        quarter = half // 2
        for side in range(2):
            first = (1 + side) * pair
            to = lane((1, LANES - 1)[side])
            at = pl.ds(pl.multiple_of(core * half + side * quarter, quarter), quarter)
            found.append(
                weight_copy(
                    entry.at[at, first : first + pair], entry.at[at, 3 * pair :], 6 + side * 2, to
                )
            )
            found.append(
                weight_copy(
                    exit_rows.at[exit_at(1 + side, units // 4, side)],
                    exit_rows.at[exit_at(3, units // 4, side)],
                    7 + side * 2,
                    to,
                )
            )
        return found

    def chip_weights(far):
        columns = slice(3 * pair, 4 * pair) if far else slice(pair, 3 * pair)
        place_in = entry.at[own_half, columns]
        found = [weight_copy(place_in, place_in, 10 + far, (partner, me))]
        for slot in (3,) if far else (1, 2):
            block = exit_rows.at[exit_at(slot, units // 2, 0)]
            found.append(weight_copy(block, block, 11 + slot, (partner, me)))
        return found

    for copy in near_weights():
        copy.start()
    for copy in row_copies:
        copy.wait()
    local.wait()

    lanes_at = iota((SPAN, 128), 1)
    front = lax.rem(lanes_at, HEAD_DIM) < HEAD_DIM // 2
    first_head = lanes_at < HEAD_DIM
    token_rows = all_rows[...]

    def turned(piece):
        other = jnp.where(
            front, -pltpu.roll(piece, 128 - HEAD_DIM // 2, 1), pltpu.roll(piece, HEAD_DIM // 2, 1)
        )
        return piece * cosine + other * sine

    ready("query", "key", "value")
    projected = dot(token_rows, query_ref[...])
    zero = jnp.zeros((SPAN, 128), float32)
    for group in range(2):
        piece = turned(projected[:, group * 128 : (group + 1) * 128]).astype(bfloat16).astype(float32)
        piece = piece * HEAD_DIM ** (-0.5)
        swapped = pltpu.roll(piece, HEAD_DIM, 1)
        keep = first_head if group == 0 else jnp.logical_not(first_head)
        members = (piece, swapped) if group == 0 else (swapped, piece)
        for member in range(2):
            at = (group * 2 + member) * SPAN
            stacked[at : at + SPAN, :] = jnp.where(keep, members[member], zero).astype(bfloat16)
    new_keys = turned(dot(token_rows, key_ref[...])).astype(bfloat16)
    new_values = dot(token_rows, value_ref[...]).astype(bfloat16)
    heads = 4 * SPAN
    causal = iota((heads, SPAN), 1) <= lax.rem(iota((heads, SPAN), 0), SPAN)
    expo = jnp.where(causal, jnp.exp(dot_last(stacked[...], new_keys)), 0.0)
    numerator[...] = dot(expo.astype(bfloat16), new_values)
    denominator[...] = jnp.sum(expo, axis=-1, keepdims=True)
    ready("keys", "values")

    @pl.loop(0, keys_ref.shape[0] // key_block)
    def _(number):
        at = pl.ds(pl.multiple_of(number * key_block, key_block), key_block)
        scores = dot_last(stacked[...], keys_ref[at, :])
        inside = iota((heads, key_block), 1) < length - number * key_block
        block = jnp.where(inside, jnp.exp(scores), 0.0)
        numerator[...] += dot(block.astype(bfloat16), values_ref[at, :])
        denominator[...] += jnp.sum(block, axis=-1, keepdims=True)

    ready("out")
    mean_values = numerator[...] / denominator[...]
    head = [mean_values[at * SPAN : (at + 1) * SPAN] for at in range(4)]
    attended = jnp.concatenate(
        [
            jnp.where(first_head, head[0], pltpu.roll(head[1], HEAD_DIM, 1)),
            jnp.where(first_head, pltpu.roll(head[2], HEAD_DIM, 1), head[3]),
        ],
        axis=1,
    ).astype(bfloat16)
    part[...] = dot(attended, out_ref[...]).astype(bfloat16)

    mix_copies = []
    for step in range(1, LANES):
        other = lax.rem(me + step, LANES)
        mix_copies.append(
            send(
                part.at[pl.ds(pl.multiple_of(other * rows, rows), rows)],
                part_held.at[step - 1],
                mix_send.at[step - 1],
                mix_recv.at[step - 1],
                (req, other),
            )
        )
    for copy in mix_copies:
        copy.start()
    for copy in near_weights():
        copy.wait()
    for copy in far_weights() + chip_weights(False):
        copy.start()
    total = part[own_place, :].astype(float32)
    for step, copy in enumerate(mix_copies):
        copy.wait()
        total = total + part_held[step].astype(float32)
    ready("expert_gain", "router", "routes")
    mixed = (own_ref[...].astype(float32) + total).astype(bfloat16)
    expert_in = rms_scale(mixed, expert_gain_ref[...]).astype(bfloat16)

    expert_at = iota((EXPERTS, SPAN), 0)
    every_named = jnp.zeros((EXPERTS, SPAN), float32)
    for choice in range(TOPK):
        every_named = every_named + jnp.where(routes_ref[choice : choice + 1, :] == expert_at, 1.0, 0.0)
    own_tokens = one_hot(iota((rows, SPAN), 1) == iota((rows, SPAN), 0) + me * rows)
    named = dot_last(own_tokens, every_named.astype(bfloat16))
    gate_expo = jnp.where(named > 0.0, jnp.exp(dot_last(expert_in, router_ref[...])), 0.0)
    gate_values = (gate_expo / jnp.sum(gate_expo, axis=-1, keepdims=True)).astype(bfloat16)
    earlier = one_hot(iota((rows, rows), 1) < iota((rows, rows), 0))
    ranks = jnp.where(named > 0.0, dot(earlier, named.astype(bfloat16)), 99.0).astype(bfloat16)
    slots = EXPERTS * SLOT_ROWS
    spread = one_hot(iota((slots, EXPERTS), 0) // SLOT_ROWS == iota((slots, EXPERTS), 1))
    slot_rank = dot_last(spread, ranks)
    slot_row = lax.rem(iota((slots, rows), 0), SLOT_ROWS)
    chunks = PACKED // CHUNK

    def picker(chunk):
        return one_hot(slot_rank == packed_rank(slot_row, chunk).astype(float32))

    main = picker(None)
    for chunk in range(chunks):
        span = slice(chunk * CHUNK, (chunk + 1) * CHUNK)
        piece = dot(main, expert_in[:, span]) + dot(picker(chunk), expert_in[:, PACKED:])
        outgoing[:, :, span] = piece.astype(bfloat16).reshape(EXPERTS, SLOT_ROWS, CHUNK)

    def target(step):
        far, near = step // 4, lax.rem(step, 4)
        to_z = lax.rem(z + far, RING_Z)
        sign = 1 - 2 * lax.rem(y + near, 2)
        to_y = lax.rem(y + sign * near + RING_Y, RING_Y)
        return to_z * RING_Y + to_y

    def origin(step):
        far, near = step // 4, lax.rem(step, 4)
        from_z = lax.rem(z - far + RING_Z, RING_Z)
        sign = 1 - 2 * lax.rem(y, 2)
        from_y = lax.rem(y - sign * near + RING_Y, RING_Y)
        return from_z * RING_Y + from_y

    def go_copy(step):
        to = target(step)
        return send(
            outgoing.at[to // 2], arrived.at[step], go_send.at[step], go_recv.at[step], (to * 2 + core, me)
        )

    def return_copy(step):
        return send(
            result.at[step],
            back.at[mine],
            ret_send.at[step],
            ret_recv.at[step],
            (origin(step) * 2 + core, me),
        )

    own_block = pltpu.make_async_copy(outgoing.at[mine], arrived.at[0], local_sem.at[1])
    own_block.start()

    @pl.loop(1, experts)
    def _(step):
        go_copy(step).start()

    own_block.wait()
    for copy in far_weights():
        copy.wait()
    for copy in chip_weights(True):
        copy.start()
    for copy in chip_weights(False) + chip_weights(True):
        copy.wait()

    ready("gate", "up", "down")
    group = 8
    group_rows = group * SLOT_ROWS
    row_at, column_at = iota((group_rows, group_rows), 0), iota((group_rows, group_rows), 1)
    same_slot = row_at // SLOT_ROWS == column_at // SLOT_ROWS
    row_in, column_in = lax.rem(row_at, SLOT_ROWS), lax.rem(column_at, SLOT_ROWS)
    kept = one_hot(same_slot & (packed_rank(row_in, None) == column_in))
    packs = [one_hot(same_slot & (packed_rank(row_in, chunk) == column_in)) for chunk in range(chunks)]
    unpacks = [one_hot(same_slot & (packed_rank(column_in, chunk) == row_in)) for chunk in range(chunks)]

    @pl.loop(0, experts // group)
    def _(number):
        first = number * group
        for offset in range(group):
            step = first + offset

            @pl.when(step > 0)
            def _():
                go_copy(step).wait_recv()

        block = arrived[pl.ds(first, group)].reshape(group_rows, PACKED)
        end = None
        for chunk in range(chunks):
            moved = dot(unpacks[chunk], block[:, chunk * CHUNK : (chunk + 1) * CHUNK])
            end = moved if end is None else end + moved
        whole = jnp.concatenate([block, end.astype(bfloat16)], axis=1)
        entered = dot(whole, entry[...])
        hidden = []
        for held in range(LANES):
            gate_part = entered[:, held * pair : held * pair + units]
            up_part = entered[:, held * pair + units : (held + 1) * pair]
            hidden.append((gate_part / (1.0 + jnp.exp(-gate_part)) * up_part).astype(bfloat16))
        total = dot(jnp.concatenate(hidden, axis=1), exit_rows[...])
        rounded = total.astype(bfloat16)
        for chunk in range(chunks):
            span = slice(chunk * CHUNK, (chunk + 1) * CHUNK)
            piece = dot(kept, rounded[:, span]) + dot(packs[chunk], rounded[:, PACKED:])
            result[pl.ds(first, group), :, span] = piece.astype(bfloat16).reshape(
                group, SLOT_ROWS, CHUNK
            )
        for offset in range(group):
            step = first + offset

            @pl.when(step > 0)
            def _():
                return_copy(step).start()

    own_back = pltpu.make_async_copy(result.at[0], back.at[mine], local_sem.at[2])
    own_back.start()
    wide_spread = one_hot(iota((EXPERTS, slots), 1) // SLOT_ROWS == iota((EXPERTS, slots), 0))
    row_rank = dot(ranks, wide_spread)
    row_gate = dot(gate_values, wide_spread)
    slot_column = lax.rem(iota((rows, slots), 1), SLOT_ROWS)

    def combine(chunk):
        found = row_rank == packed_rank(slot_column, chunk).astype(float32)
        return jnp.where(found, row_gate, 0.0).astype(bfloat16)

    main = combine(None)
    ends = [combine(chunk) for chunk in range(chunks)]
    own_back.wait()

    @pl.loop(1, experts)
    def _(step):
        return_copy(step).wait_recv()

    end = None
    sums = []
    for chunk in range(chunks):
        piece = back[:, :, chunk * CHUNK : (chunk + 1) * CHUNK].reshape(slots, CHUNK)
        sums.append(dot(main, piece))
        moved = dot(ends[chunk], piece)
        end = moved if end is None else end + moved
    sums.append(end)
    layer = (mixed.astype(float32) + jnp.concatenate(sums, axis=1)).astype(bfloat16)
    layer_ref[...] = layer
    parts = width // 128
    closing = layer[rows - 8 :, :].astype(float32)
    tail[...] = jnp.concatenate(
        [closing[7:8, at * 128 : (at + 1) * 128] for at in range(parts)], axis=0
    ).astype(bfloat16)

    def lane_copy(to):
        return send(tail, tails.at[core, place], lane_send.at[to], lane_recv, (req, to))

    @pl.when(me == last)
    def _():
        for to in range(last):
            lane_copy(to).start()
        own = pltpu.make_async_copy(tail, tails.at[core, place], local_sem.at[3])
        own.start()
        own.wait()
        for to in range(last):
            lane_copy(to).wait_send()

    @pl.when(me != last)
    def _():
        send(tail, tails.at[core, place], lane_send.at[0], lane_recv, (req, last)).wait_recv()

    def plane_copy(step):
        own_row = tails.at[core, place]
        return send(own_row, own_row, plane_send.at[step], plane_recv.at[step], plane_peer(step))

    @pl.loop(1, places)
    def _(step):
        plane_copy(step).start()

    @pl.loop(1, experts)
    def _(step):
        go_copy(step).wait_send()
        return_copy(step).wait_send()

    @pl.loop(1, places)
    def _(step):
        plane_copy(step).wait()

    other_half = send(tails.at[core], tails.at[core], core_sem.at[0], core_sem.at[1], (partner, me))
    other_half.start()
    other_half.wait()

    ready("final_gain", "order", "vocab")
    count = 2 * places
    tails_wide[...] = tails[...].astype(float32).reshape(count, parts, 128)
    square = jnp.zeros((count, 1), float32)
    for at in range(parts):
        piece = tails_wide[:, at, :]
        square = square + jnp.sum(piece * piece, axis=-1, keepdims=True)
    scale = lax.rsqrt(square / width + epsilon)
    by_slot = one_hot(iota((count, count), 0) == order_ref[...])
    slot_at, held_at = iota((count, count), 0), iota((count, count), 1)
    held_slot = lax.rem(held_at, places) * 2 + held_at // places
    chosen = dot(by_slot, one_hot(slot_at == held_slot)).astype(bfloat16)
    found = jnp.zeros(logits_ref.shape, float32)
    for at in range(parts):
        span = slice(at * 128, (at + 1) * 128)
        final = (tails_wide[:, at, :] * scale * final_gain_ref[:, span]).astype(bfloat16)
        ordered = dot(chosen, final).astype(bfloat16)
        found = found + dot_last(vocab_ref[:, span], ordered)
    logits_ref[...] = found


def body(
    hidden_in,
    cache_keys,
    cache_values,
    lengths,
    request_order,
    routes,
    query_weight,
    key_weight,
    value_weight,
    out_weight,
    attention_gain,
    expert_gain,
    router_weight,
    gate_weight,
    up_weight,
    down_weight,
    final_gain,
    vocab_weight,
):
    own_rows = hidden_in[0]
    rows, width = own_rows.shape
    units = gate_weight.shape[2]
    reqs = lengths.shape[0]
    places = reqs // 2
    half_dim = HEAD_DIM // 2
    frequency = np.exp(-np.log(10000.0) * np.arange(half_dim) * (2.0 / HEAD_DIM)).astype(np.float32)
    frequency = jnp.asarray(np.tile(frequency, 128 // half_dim)[None, :])
    operands = [
        lengths,
        own_rows,
        cache_keys[0],
        cache_values[0],
        routes[0].T,
        query_weight,
        key_weight,
        value_weight,
        out_weight,
        attention_gain.reshape(1, width),
        expert_gain.reshape(1, width),
        router_weight.T,
        gate_weight[0],
        up_weight[0],
        down_weight[0],
        final_gain.reshape(1, width),
        request_order.reshape(1, reqs),
        vocab_weight.T,
    ]
    dma = pltpu.SemaphoreType.DMA
    heads = 4 * SPAN
    slot_block = pltpu.VMEM((EXPERTS, SLOT_ROWS, PACKED), bfloat16)
    layer_rows, logits = pl.pallas_call(
        layer_kernel,
        out_shape=[
            jax.ShapeDtypeStruct((rows, width), bfloat16),
            jax.ShapeDtypeStruct((vocab_weight.shape[1], reqs), float32),
        ],
        in_specs=[VMEM_SPEC] + [pl.BlockSpec(memory_space=pltpu.HBM)] * len(operands),
        out_specs=[VMEM_SPEC] * 2,
        scratch_shapes=[pltpu.SMEM((reqs,), jnp.int32)]
        + [pltpu.VMEM(operand.shape, operand.dtype) for operand in operands[1:12] + operands[15:]]
        + [
            pltpu.VMEM((rows, width), bfloat16),
            pltpu.VMEM((SPAN, width), bfloat16),
            pltpu.VMEM((heads, 128), bfloat16),
            pltpu.VMEM((heads, 128), float32),
            pltpu.VMEM((heads, 1), float32),
            pltpu.VMEM((SPAN, width), bfloat16),
            pltpu.VMEM((LANES - 1, rows, width), bfloat16),
            slot_block,
            slot_block,
            slot_block,
            slot_block,
            pltpu.VMEM((width, LANES * 2 * units), bfloat16),
            pltpu.VMEM((LANES * units, width), bfloat16),
            pltpu.VMEM((width // 128, 128), bfloat16),
            pltpu.VMEM((2, places, width // 128, 128), bfloat16),
            pltpu.VMEM((reqs, width // 128, 128), float32),
            dma((LANES - 1,)),
            dma((LANES - 1,)),
            dma((LANES - 1,)),
            dma((LANES - 1,)),
            dma((15,)),
            dma((15,)),
            dma((EXPERTS,)),
            dma((EXPERTS,)),
            dma((EXPERTS,)),
            dma((EXPERTS,)),
            dma((LANES - 1,)),
            dma,
            dma((places,)),
            dma((places,)),
            dma((2,)),
            dma((4,)),
            dma((len(operands),)),
        ],
        compiler_params=pltpu.CompilerParams(
            collective_id=0, has_side_effects=True, vmem_limit_bytes=67043328
        ),
        name="layer",
    )(frequency, *operands)
    return (layer_rows[None], logits.T)


def solution(mesh):
    in_specs = (
        P("req", "tp", None),
        P("req", None, "tp"),
        P("req", None, "tp"),
        P(),
        P(),
        P("req", None, None),
        P(None, "tp"),
        P(None, "tp"),
        P(None, "tp"),
        P("tp", None),
        P(),
        P(),
        P(),
        P("req", None, "tp"),
        P("req", None, "tp"),
        P("req", "tp", None),
        P(),
        P(None, ("req", "tp")),
    )
    out_specs = (P("req", "tp", None), P(None, ("req", "tp")))
    return jax.shard_map(body, mesh=mesh, in_specs=in_specs, out_specs=out_specs, check_vma=False)
```

```python
import jax
import jax.numpy as jnp
import numpy as np
from jax.experimental import pallas as pl
from jax.experimental.pallas import tpu as pltpu
from jax import lax
from jax.sharding import PartitionSpec as P

HEAD_DIM = 64
EXPERTS = 32
TOPK = 8
LANES = 4
RING_Y = 8
RING_Z = 8
SPAN = 128
SLOT_ROWS = 16
CAP = 12
PACKED = 768
CHUNK = 256
MESH = pl.DeviceIdType.MESH
VMEM_SPEC = pl.BlockSpec(memory_space=pltpu.VMEM)


epsilon = 1e-06
key_block = 512
float32 = jnp.float32
bfloat16 = jnp.bfloat16


def rms_scale(row_block, gain_vector):
    widened = row_block.astype(jnp.float32)
    return (
        widened
        * lax.rsqrt(jnp.mean(widened * widened, axis=-1, keepdims=True) + epsilon)
        * gain_vector
    )


def send(source, target, send_sem, recv_sem, device):
    return pltpu.make_async_remote_copy(
        src_ref=source,
        dst_ref=target,
        send_sem=send_sem,
        recv_sem=recv_sem,
        device_id=device,
        device_id_type=MESH,
    )


def greet(barrier, device):
    pl.semaphore_signal(barrier, inc=1, device_id=device, device_id_type=MESH)


def dot(a, b):
    return jnp.dot(a, b, preferred_element_type=float32)


def dot_last(a, b):
    return lax.dot_general(a, b, (((1,), (1,)), ((), ())), preferred_element_type=float32)


def iota(shape, axis):
    return lax.broadcasted_iota(jnp.int32, shape, axis)


def one_hot(mask):
    return jnp.where(mask, 1.0, 0.0).astype(bfloat16)


def packed_rank(slot_row, chunk):
    if chunk is None:
        return jnp.where(slot_row < CAP, slot_row, -1)
    return jnp.where(slot_row >= CAP, slot_row - CAP + (SLOT_ROWS - CAP) * chunk, -1)


def layer_kernel(
    frequency_ref,
    length_hbm,
    own_hbm,
    keys_hbm,
    values_hbm,
    routes_hbm,
    query_hbm,
    key_hbm,
    value_hbm,
    out_hbm,
    attention_gain_hbm,
    expert_gain_hbm,
    router_hbm,
    gate_hbm,
    up_hbm,
    down_hbm,
    final_gain_hbm,
    order_hbm,
    vocab_hbm,
    layer_ref,
    logits_ref,
    length_ref,
    own_ref,
    keys_ref,
    values_ref,
    routes_ref,
    query_ref,
    key_ref,
    value_ref,
    out_ref,
    attention_gain_ref,
    expert_gain_ref,
    router_ref,
    final_gain_ref,
    order_ref,
    vocab_ref,
    normed,
    all_rows,
    stacked,
    numerator,
    denominator,
    part,
    part_held,
    outgoing,
    arrived,
    result,
    back,
    entry,
    exit_rows,
    tail,
    tails,
    tails_wide,
    row_send,
    row_recv,
    mix_send,
    mix_recv,
    weight_send,
    weight_recv,
    go_send,
    go_recv,
    ret_send,
    ret_recv,
    lane_send,
    lane_recv,
    plane_send,
    plane_recv,
    core_sem,
    local_sem,
    load_sem,
):
    req, me = lax.axis_index("req"), lax.axis_index("tp")
    z, y, core = req // (2 * RING_Y), lax.rem(req // 2, RING_Y), lax.rem(req, 2)
    place = req // 2
    places = RING_Y * RING_Z
    mine = place // 2
    experts, _, _ = outgoing.shape
    rows, width = own_ref.shape
    units = down_hbm.shape[0]
    pair = 2 * units
    partner = z * 2 * RING_Y + y * 2 + 1 - core
    last = LANES - 1
    barrier = pltpu.get_barrier_semaphore()

    def lane(step):
        return (req, lax.rem(me + step, LANES))

    def plane_peer(step):
        return (lax.rem(place + step, places) * 2 + core, me)

    for step in range(1, LANES):
        greet(barrier, lane(step))
    greet(barrier, (partner, me))

    @pl.loop(1, places)
    def _(step):
        greet(barrier, plane_peer(step))

    loads = {}
    for number, (name, source, held) in enumerate(
        (
            ("own", own_hbm, own_ref),
            ("attention_gain", attention_gain_hbm, attention_gain_ref),
            ("length", length_hbm, length_ref),
            ("keys", keys_hbm, keys_ref),
            ("values", values_hbm, values_ref),
            ("routes", routes_hbm, routes_ref),
            ("query", query_hbm, query_ref),
            ("key", key_hbm, key_ref),
            ("value", value_hbm, value_ref),
            ("out", out_hbm, out_ref),
            ("expert_gain", expert_gain_hbm, expert_gain_ref),
            ("router", router_hbm, router_ref),
            ("gate", gate_hbm, entry.at[:, :units]),
            ("up", up_hbm, entry.at[:, units : 2 * units]),
            ("down", down_hbm, exit_rows.at[:units]),
            ("final_gain", final_gain_hbm, final_gain_ref),
            ("order", order_hbm, order_ref),
            ("vocab", vocab_hbm, vocab_ref),
        )
    ):
        loads[name] = pltpu.make_async_copy(source, held, load_sem.at[number])
        loads[name].start()

    def ready(*wanted):
        for name in wanted:
            loads[name].wait()

    ready("own", "attention_gain", "length")
    normed[...] = rms_scale(own_ref[...], attention_gain_ref[...]).astype(bfloat16)
    own_place = pl.ds(pl.multiple_of(me * rows, rows), rows)
    local = pltpu.make_async_copy(normed, all_rows.at[own_place], local_sem.at[0])
    local.start()
    length = length_ref[req]
    positions = (length + iota((SPAN, 128), 0)).astype(float32)
    angles = positions * frequency_ref[...]
    cosine, sine = jnp.cos(angles), jnp.sin(angles)
    ready("routes", "order")
    expert_at = iota((EXPERTS, SPAN), 0)
    every_named = jnp.zeros((EXPERTS, SPAN), float32)
    for choice in range(TOPK):
        every_named = every_named + jnp.where(routes_ref[choice : choice + 1, :] == expert_at, 1.0, 0.0)
    own_tokens = one_hot(iota((rows, SPAN), 1) == iota((rows, SPAN), 0) + me * rows)
    named = dot_last(own_tokens, every_named.astype(bfloat16))
    earlier = one_hot(iota((rows, rows), 1) < iota((rows, rows), 0))
    ranks = jnp.where(named > 0.0, dot(earlier, named.astype(bfloat16)), 99.0).astype(bfloat16)
    slots = EXPERTS * SLOT_ROWS
    spread = one_hot(iota((slots, EXPERTS), 0) // SLOT_ROWS == iota((slots, EXPERTS), 1))
    slot_rank = dot_last(spread, ranks)
    slot_row = lax.rem(iota((slots, rows), 0), SLOT_ROWS)
    chunks = PACKED // CHUNK

    def picker(chunk):
        return one_hot(slot_rank == packed_rank(slot_row, chunk).astype(float32))

    main_picker = picker(None)
    end_pickers = [picker(chunk) for chunk in range(chunks)]
    group = 8
    group_rows = group * SLOT_ROWS
    row_at, column_at = iota((group_rows, group_rows), 0), iota((group_rows, group_rows), 1)
    same_slot = row_at // SLOT_ROWS == column_at // SLOT_ROWS
    row_in, column_in = lax.rem(row_at, SLOT_ROWS), lax.rem(column_at, SLOT_ROWS)
    kept = one_hot(same_slot & (packed_rank(row_in, None) == column_in))
    packs = [one_hot(same_slot & (packed_rank(row_in, chunk) == column_in)) for chunk in range(chunks)]
    unpacks = [one_hot(same_slot & (packed_rank(column_in, chunk) == row_in)) for chunk in range(chunks)]

    count = 2 * places
    by_slot = one_hot(iota((count, count), 0) == order_ref[...])
    slot_at, held_at = iota((count, count), 0), iota((count, count), 1)
    held_slot = lax.rem(held_at, places) * 2 + held_at // places
    chosen = dot(by_slot, one_hot(slot_at == held_slot)).astype(bfloat16)
    pl.semaphore_wait(barrier, LANES - 1 + 1 + places - 1)

    row_copies = [
        send(normed, all_rows.at[own_place], row_send.at[step - 1], row_recv.at[step - 1], lane(step))
        for step in range(1, LANES)
    ]
    for copy in row_copies:
        copy.start()
    half = width // 2
    own_half = pl.ds(pl.multiple_of(core * half, half), half)

    def exit_at(slot, amount, side):
        first = slot * units + core * (units // 2) + side * amount
        return pl.ds(pl.multiple_of(first, amount), amount)

    def weight_copy(source, target, number, device):
        return send(source, target, weight_send.at[number], weight_recv.at[number], device)

    def near_weights():
        found = []
        for side in range(2):
            first = (1 + side) * pair
            to = lane((1, LANES - 1)[side])
            unit_half = pl.ds(pl.multiple_of(core * (units // 2), units // 2), units // 2)
            for number, (source, target) in enumerate(
                (
                    (gate_hbm.at[own_half], entry.at[own_half, first : first + units]),
                    (up_hbm.at[own_half], entry.at[own_half, first + units : first + pair]),
                    (down_hbm.at[unit_half], exit_rows.at[exit_at(1 + side, units // 2, 0)]),
                )
            ):
                found.append(weight_copy(source, target, side * 3 + number, to))
        return found

    def far_weights():
        found = []
        quarter = half // 2
        for side in range(2):
            first = (1 + side) * pair
            to = lane((1, LANES - 1)[side])
            at = pl.ds(pl.multiple_of(core * half + side * quarter, quarter), quarter)
            found.append(
                weight_copy(
                    entry.at[at, first : first + pair], entry.at[at, 3 * pair :], 6 + side * 2, to
                )
            )
            found.append(
                weight_copy(
                    exit_rows.at[exit_at(1 + side, units // 4, side)],
                    exit_rows.at[exit_at(3, units // 4, side)],
                    7 + side * 2,
                    to,
                )
            )
        return found

    def chip_weights(far):
        columns = slice(3 * pair, 4 * pair) if far else slice(pair, 3 * pair)
        place_in = entry.at[own_half, columns]
        found = [weight_copy(place_in, place_in, 10 + far, (partner, me))]
        for slot in (3,) if far else (1, 2):
            block = exit_rows.at[exit_at(slot, units // 2, 0)]
            found.append(weight_copy(block, block, 11 + slot, (partner, me)))
        return found

    for copy in near_weights():
        copy.start()
    for copy in row_copies:
        copy.wait()
    local.wait()

    lanes_at = iota((SPAN, 128), 1)
    front = lax.rem(lanes_at, HEAD_DIM) < HEAD_DIM // 2
    first_head = lanes_at < HEAD_DIM
    token_rows = all_rows[...]

    def turned(piece):
        other = jnp.where(
            front, -pltpu.roll(piece, 128 - HEAD_DIM // 2, 1), pltpu.roll(piece, HEAD_DIM // 2, 1)
        )
        return piece * cosine + other * sine

    ready("query", "key", "value")
    projected = dot(token_rows, query_ref[...])
    zero = jnp.zeros((SPAN, 128), float32)
    for block_at in range(2):
        piece = turned(projected[:, block_at * 128 : (block_at + 1) * 128]).astype(bfloat16).astype(float32)
        piece = piece * HEAD_DIM ** (-0.5)
        swapped = pltpu.roll(piece, HEAD_DIM, 1)
        keep = first_head if block_at == 0 else jnp.logical_not(first_head)
        members = (piece, swapped) if block_at == 0 else (swapped, piece)
        for member in range(2):
            at = (block_at * 2 + member) * SPAN
            stacked[at : at + SPAN, :] = jnp.where(keep, members[member], zero).astype(bfloat16)
    new_keys = turned(dot(token_rows, key_ref[...])).astype(bfloat16)
    new_values = dot(token_rows, value_ref[...]).astype(bfloat16)
    heads = 4 * SPAN
    causal = iota((heads, SPAN), 1) <= lax.rem(iota((heads, SPAN), 0), SPAN)
    expo = jnp.where(causal, jnp.exp(dot_last(stacked[...], new_keys)), 0.0)
    numerator[...] = dot(expo.astype(bfloat16), new_values)
    denominator[...] = jnp.sum(expo, axis=-1, keepdims=True)
    ready("keys", "values")

    @pl.loop(0, keys_ref.shape[0] // key_block)
    def _(number):
        at = pl.ds(pl.multiple_of(number * key_block, key_block), key_block)
        scores = dot_last(stacked[...], keys_ref[at, :])
        inside = iota((heads, key_block), 1) < length - number * key_block
        block = jnp.where(inside, jnp.exp(scores), 0.0)
        numerator[...] += dot(block.astype(bfloat16), values_ref[at, :])
        denominator[...] += jnp.sum(block, axis=-1, keepdims=True)

    ready("out")
    mean_values = numerator[...] / denominator[...]
    head = [mean_values[at * SPAN : (at + 1) * SPAN] for at in range(4)]
    attended = jnp.concatenate(
        [
            jnp.where(first_head, head[0], pltpu.roll(head[1], HEAD_DIM, 1)),
            jnp.where(first_head, pltpu.roll(head[2], HEAD_DIM, 1), head[3]),
        ],
        axis=1,
    ).astype(bfloat16)
    part[...] = dot(attended, out_ref[...]).astype(bfloat16)

    mix_copies = []
    for step in range(1, LANES):
        other = lax.rem(me + step, LANES)
        mix_copies.append(
            send(
                part.at[pl.ds(pl.multiple_of(other * rows, rows), rows)],
                part_held.at[step - 1],
                mix_send.at[step - 1],
                mix_recv.at[step - 1],
                (req, other),
            )
        )
    for copy in mix_copies:
        copy.start()
    for copy in near_weights():
        copy.wait()
    for copy in far_weights() + chip_weights(False):
        copy.start()
    total = part[own_place, :].astype(float32)
    for step, copy in enumerate(mix_copies):
        copy.wait()
        total = total + part_held[step].astype(float32)
    ready("expert_gain", "router")
    mixed = (own_ref[...].astype(float32) + total).astype(bfloat16)
    expert_in = rms_scale(mixed, expert_gain_ref[...]).astype(bfloat16)

    gate_expo = jnp.where(named > 0.0, jnp.exp(dot_last(expert_in, router_ref[...])), 0.0)
    gate_values = (gate_expo / jnp.sum(gate_expo, axis=-1, keepdims=True)).astype(bfloat16)
    for chunk in range(chunks):
        span = slice(chunk * CHUNK, (chunk + 1) * CHUNK)
        piece = dot(main_picker, expert_in[:, span]) + dot(end_pickers[chunk], expert_in[:, PACKED:])
        outgoing[:, :, span] = piece.astype(bfloat16).reshape(EXPERTS, SLOT_ROWS, CHUNK)

    def target(step):
        far, near = step // 4, lax.rem(step, 4)
        to_z = lax.rem(z + far, RING_Z)
        sign = 1 - 2 * lax.rem(y + near, 2)
        to_y = lax.rem(y + sign * near + RING_Y, RING_Y)
        return to_z * RING_Y + to_y

    def origin(step):
        far, near = step // 4, lax.rem(step, 4)
        from_z = lax.rem(z - far + RING_Z, RING_Z)
        sign = 1 - 2 * lax.rem(y, 2)
        from_y = lax.rem(y - sign * near + RING_Y, RING_Y)
        return from_z * RING_Y + from_y

    def go_copy(step):
        to = target(step)
        return send(
            outgoing.at[to // 2], arrived.at[step], go_send.at[step], go_recv.at[step], (to * 2 + core, me)
        )

    def return_copy(step):
        return send(
            result.at[step],
            back.at[mine],
            ret_send.at[step],
            ret_recv.at[step],
            (origin(step) * 2 + core, me),
        )

    own_block = pltpu.make_async_copy(outgoing.at[mine], arrived.at[0], local_sem.at[1])
    own_block.start()

    @pl.loop(1, experts)
    def _(step):
        go_copy(step).start()

    own_block.wait()
    for copy in far_weights():
        copy.wait()
    for copy in chip_weights(True):
        copy.start()
    for copy in chip_weights(False) + chip_weights(True):
        copy.wait()

    ready("gate", "up", "down")
    @pl.loop(0, experts // group)
    def _(number):
        first = number * group
        for offset in range(group):
            step = first + offset

            @pl.when(step > 0)
            def _():
                go_copy(step).wait_recv()

        block = arrived[pl.ds(first, group)].reshape(group_rows, PACKED)
        end = None
        for chunk in range(chunks):
            moved = dot(unpacks[chunk], block[:, chunk * CHUNK : (chunk + 1) * CHUNK])
            end = moved if end is None else end + moved
        whole = jnp.concatenate([block, end.astype(bfloat16)], axis=1)
        entered = dot(whole, entry[...])
        hidden = []
        for held in range(LANES):
            gate_part = entered[:, held * pair : held * pair + units]
            up_part = entered[:, held * pair + units : (held + 1) * pair]
            hidden.append((gate_part / (1.0 + jnp.exp(-gate_part)) * up_part).astype(bfloat16))
        total = dot(jnp.concatenate(hidden, axis=1), exit_rows[...])
        rounded = total.astype(bfloat16)
        for chunk in range(chunks):
            span = slice(chunk * CHUNK, (chunk + 1) * CHUNK)
            piece = dot(kept, rounded[:, span]) + dot(packs[chunk], rounded[:, PACKED:])
            result[pl.ds(first, group), :, span] = piece.astype(bfloat16).reshape(
                group, SLOT_ROWS, CHUNK
            )
        for offset in range(group):
            step = first + offset

            @pl.when(step > 0)
            def _():
                return_copy(step).start()

    own_back = pltpu.make_async_copy(result.at[0], back.at[mine], local_sem.at[2])
    own_back.start()
    wide_spread = one_hot(iota((EXPERTS, slots), 1) // SLOT_ROWS == iota((EXPERTS, slots), 0))
    row_rank = dot(ranks, wide_spread)
    row_gate = dot(gate_values, wide_spread)
    slot_column = lax.rem(iota((rows, slots), 1), SLOT_ROWS)

    def combine(chunk):
        found = row_rank == packed_rank(slot_column, chunk).astype(float32)
        return jnp.where(found, row_gate, 0.0).astype(bfloat16)

    main = combine(None)
    ends = [combine(chunk) for chunk in range(chunks)]
    own_back.wait()

    @pl.loop(1, experts)
    def _(step):
        return_copy(step).wait_recv()

    end = None
    sums = []
    for chunk in range(chunks):
        piece = back[:, :, chunk * CHUNK : (chunk + 1) * CHUNK].reshape(slots, CHUNK)
        sums.append(dot(main, piece))
        moved = dot(ends[chunk], piece)
        end = moved if end is None else end + moved
    sums.append(end)
    layer = (mixed.astype(float32) + jnp.concatenate(sums, axis=1)).astype(bfloat16)
    layer_ref[...] = layer
    parts = width // 128
    closing = layer[rows - 8 :, :].astype(float32)
    tail[...] = jnp.concatenate(
        [closing[7:8, at * 128 : (at + 1) * 128] for at in range(parts)], axis=0
    ).astype(bfloat16)

    def lane_copy(to):
        return send(tail, tails.at[core, place], lane_send.at[to], lane_recv, (req, to))

    @pl.when(me == last)
    def _():
        for to in range(last):
            lane_copy(to).start()
        own = pltpu.make_async_copy(tail, tails.at[core, place], local_sem.at[3])
        own.start()
        own.wait()
        for to in range(last):
            lane_copy(to).wait_send()

    @pl.when(me != last)
    def _():
        send(tail, tails.at[core, place], lane_send.at[0], lane_recv, (req, last)).wait_recv()

    def plane_copy(step):
        own_row = tails.at[core, place]
        return send(own_row, own_row, plane_send.at[step], plane_recv.at[step], plane_peer(step))

    @pl.loop(1, places)
    def _(step):
        plane_copy(step).start()

    @pl.loop(1, experts)
    def _(step):
        go_copy(step).wait_send()
        return_copy(step).wait_send()

    @pl.loop(1, places)
    def _(step):
        plane_copy(step).wait()

    other_half = send(tails.at[core], tails.at[core], core_sem.at[0], core_sem.at[1], (partner, me))
    other_half.start()
    other_half.wait()

    ready("final_gain", "vocab")
    tails_wide[...] = tails[...].astype(float32).reshape(count, parts, 128)
    square = jnp.zeros((count, 1), float32)
    for at in range(parts):
        piece = tails_wide[:, at, :]
        square = square + jnp.sum(piece * piece, axis=-1, keepdims=True)
    scale = lax.rsqrt(square / width + epsilon)
    found = jnp.zeros(logits_ref.shape, float32)
    for at in range(parts):
        span = slice(at * 128, (at + 1) * 128)
        final = (tails_wide[:, at, :] * scale * final_gain_ref[:, span]).astype(bfloat16)
        ordered = dot(chosen, final).astype(bfloat16)
        found = found + dot_last(vocab_ref[:, span], ordered)
    logits_ref[...] = found


def body(
    hidden_in,
    cache_keys,
    cache_values,
    lengths,
    request_order,
    routes,
    query_weight,
    key_weight,
    value_weight,
    out_weight,
    attention_gain,
    expert_gain,
    router_weight,
    gate_weight,
    up_weight,
    down_weight,
    final_gain,
    vocab_weight,
):
    own_rows = hidden_in[0]
    rows, width = own_rows.shape
    units = gate_weight.shape[2]
    reqs = lengths.shape[0]
    places = reqs // 2
    half_dim = HEAD_DIM // 2
    frequency = np.exp(-np.log(10000.0) * np.arange(half_dim) * (2.0 / HEAD_DIM)).astype(np.float32)
    frequency = jnp.asarray(np.tile(frequency, 128 // half_dim)[None, :])
    operands = [
        lengths,
        own_rows,
        cache_keys[0],
        cache_values[0],
        routes[0].T,
        query_weight,
        key_weight,
        value_weight,
        out_weight,
        attention_gain.reshape(1, width),
        expert_gain.reshape(1, width),
        router_weight.T,
        gate_weight[0],
        up_weight[0],
        down_weight[0],
        final_gain.reshape(1, width),
        request_order.reshape(1, reqs),
        vocab_weight.T,
    ]
    dma = pltpu.SemaphoreType.DMA
    heads = 4 * SPAN
    slot_block = pltpu.VMEM((EXPERTS, SLOT_ROWS, PACKED), bfloat16)
    layer_rows, logits = pl.pallas_call(
        layer_kernel,
        out_shape=[
            jax.ShapeDtypeStruct((rows, width), bfloat16),
            jax.ShapeDtypeStruct((vocab_weight.shape[1], reqs), float32),
        ],
        in_specs=[VMEM_SPEC] + [pl.BlockSpec(memory_space=pltpu.HBM)] * len(operands),
        out_specs=[VMEM_SPEC] * 2,
        scratch_shapes=[pltpu.SMEM((reqs,), jnp.int32)]
        + [pltpu.VMEM(operand.shape, operand.dtype) for operand in operands[1:12] + operands[15:]]
        + [
            pltpu.VMEM((rows, width), bfloat16),
            pltpu.VMEM((SPAN, width), bfloat16),
            pltpu.VMEM((heads, 128), bfloat16),
            pltpu.VMEM((heads, 128), float32),
            pltpu.VMEM((heads, 1), float32),
            pltpu.VMEM((SPAN, width), bfloat16),
            pltpu.VMEM((LANES - 1, rows, width), bfloat16),
            slot_block,
            slot_block,
            slot_block,
            slot_block,
            pltpu.VMEM((width, LANES * 2 * units), bfloat16),
            pltpu.VMEM((LANES * units, width), bfloat16),
            pltpu.VMEM((width // 128, 128), bfloat16),
            pltpu.VMEM((2, places, width // 128, 128), bfloat16),
            pltpu.VMEM((reqs, width // 128, 128), float32),
            dma((LANES - 1,)),
            dma((LANES - 1,)),
            dma((LANES - 1,)),
            dma((LANES - 1,)),
            dma((15,)),
            dma((15,)),
            dma((EXPERTS,)),
            dma((EXPERTS,)),
            dma((EXPERTS,)),
            dma((EXPERTS,)),
            dma((LANES - 1,)),
            dma,
            dma((places,)),
            dma((places,)),
            dma((2,)),
            dma((4,)),
            dma((len(operands),)),
        ],
        compiler_params=pltpu.CompilerParams(
            collective_id=0, has_side_effects=True, vmem_limit_bytes=67043328
        ),
        name="layer",
    )(frequency, *operands)
    return (layer_rows[None], logits.T)


def solution(mesh):
    in_specs = (
        P("req", "tp", None),
        P("req", None, "tp"),
        P("req", None, "tp"),
        P(),
        P(),
        P("req", None, None),
        P(None, "tp"),
        P(None, "tp"),
        P(None, "tp"),
        P("tp", None),
        P(),
        P(),
        P(),
        P("req", None, "tp"),
        P("req", None, "tp"),
        P("req", "tp", None),
        P(),
        P(None, ("req", "tp")),
    )
    out_specs = (P("req", "tp", None), P(None, ("req", "tp")))
    return jax.shard_map(body, mesh=mesh, in_specs=in_specs, out_specs=out_specs, check_vma=False)
```
